32 devices in a mesh: tx: 2 (over x), rx: 4 (over z), freq: 4 (over y, core).
Axes of the slice: x: 2, y: 2, z: 4, core: 2. Of those that a mesh axis runs over, the one named last changes fastest.
Arguments:
- spectrum: float32 [2, 8, 2048, 2048], P(None, 'freq', 'tx', 'rx'), may hold values from -6 to 6
- measured: float32 [2, 8, 2048, 2048], P(None, 'freq', 'tx', 'rx'), may hold values from -12 to 12
- wavenumber: float32 [8], replicated, may hold values from 1.5 to 3
- send_weight: float32 [2048], P('tx'), may hold values from 0.25 to 2
- hear_weight: float32 [2048], P('rx'), may hold values from 0.25 to 2
- aperture: int32 [128, 128], P('tx', 'rx'), may hold values 0 or 1
Outputs:
- updated: float32 [2, 8, 2048, 2048], P(None, 'freq', 'tx', 'rx')
- residual: float32 [2, 8, 2048, 2048], P(None, 'freq', 'tx', 'rx')
The draws below stay inside these ranges and needn't reach their ends.
Inputs may be any that keep to these rules, and one draw needn't show every extreme that they name: `aperture`: 1 marks a live tile of 16 x 16 antenna pairs, 0 a silent one.
All inputs are finite; a program needn't handle non-finite values. No bound on the sum of `aperture` on one device may be relied on, other than what follows from the above.
Results may differ from the reference program's by a relative error of at most 0.00016.
Values sent between devices are 32-bit elements; how exact they have to be, the bound alone decides.
A program may use at most 192 MiB of HBM per device.

```python
import math
import jax
import jax.numpy as jnp
from jax import lax

F = 8
NT = 2048
NR = 2048
TILE = 16
DEPTH = 8


def with_ends(values, rng, least, top_value):
    shape = values.shape
    spot = [jax.random.randint(jax.random.fold_in(rng, axis), (), 0, shape[axis]) for axis in range(len(shape))]
    values = values.at[tuple(spot)].set(least)
    longest = shape.index(max(shape))
    spot[longest] = (spot[longest] + 1) % shape[longest]
    return values.at[tuple(spot)].set(top_value)


def level_of(stream_key, extent, split, smallest, largest):
    factor_of, own = 1.0, jax.random.fold_in(stream_key, 6)
    for position, blocks in split:
        steps = jnp.exp(jax.random.uniform(jax.random.fold_in(own, position), (blocks,), jnp.float32, smallest / len(split), largest / len(split)))
        factor_of = factor_of * jnp.repeat(steps, extent[position] // blocks).reshape([-1 if axis == position else 1 for axis in range(len(extent))])
    return factor_of


def noise(key, shape, deviation, reach, pieces=(), kind=jnp.bfloat16):
    values = deviation * jax.random.normal(key, shape, jnp.float32)
    if pieces:
        values = values * level_of(key, shape, pieces, -0.22, 0.18)
    return jnp.clip(values, -reach, reach).astype(kind)


def setup_inputs(seed: int = 0) -> dict:
    streams_of = jax.random.split(jax.random.key(seed), 7)
    spectrum = noise(streams_of[0], (2, DEPTH, NT, NR), 1.0, 6.0, ((1, 4), (2, 2), (3, 4)), jnp.float32)
    measured = noise(streams_of[1], (2, F, NT, NR), 2.0, 12.0, ((1, 4), (2, 2), (3, 4)), jnp.float32)
    wavenumber = jnp.clip(jax.random.uniform(streams_of[2], (F,), jnp.float32, 1.5, 3.0), 1.5, 3.0)
    send_weight = jnp.clip(jnp.exp(math.log(2.0) - 2.0794415 * jax.random.uniform(streams_of[3], (NT,), jnp.float32) ** level_of(streams_of[3], (NT,), ((0, 2),), -0.2, 0.2)), 0.25, 2.0)
    hear_weight = jnp.clip(jnp.exp(math.log(2.0) - 2.0794415 * jax.random.uniform(streams_of[4], (NR,), jnp.float32) ** level_of(streams_of[4], (NR,), ((0, 4),), -0.2, 0.2)), 0.25, 2.0)
    aperture = with_ends((jax.random.randint(streams_of[5], (NT // TILE, NR // TILE), 0, 3) < 2).astype(jnp.int32), jax.random.fold_in(streams_of[5], 1), 0, 1)
    return dict(spectrum=spectrum, measured=measured, wavenumber=wavenumber, send_weight=send_weight, hear_weight=hear_weight, aperture=aperture)


depth_step = 2.0
step_size = 0.125
root_floor = 0.25

def wave_numbers(offset, length, total):
    indices = offset + jnp.arange(length, dtype=jnp.int32)
    signed = jnp.where(indices < total // 2, indices, indices - total)
    return 2.0 * jnp.pi / total * signed.astype(jnp.float32)

def vertical(wavenumber, waves_sent, waves_heard):
    squared = (wavenumber * wavenumber)[:, None, None]
    first_root = jnp.sqrt(jnp.maximum(squared - (waves_sent * waves_sent)[None, :, None], 0.0) + root_floor)
    second_root = jnp.sqrt(jnp.maximum(squared - (waves_heard * waves_heard)[None, None, :], 0.0) + root_floor)
    return first_root + second_root

def reference(spectrum, measured, wavenumber, send_weight, hear_weight, aperture):
    waves_sent = wave_numbers(0, NT, NT)
    waves_heard = wave_numbers(0, NR, NR)
    vertical_waves = vertical(wavenumber, waves_sent, waves_heard)
    pair_real = jnp.zeros((F, NT, NR), jnp.float32)
    pair_imag = jnp.zeros((F, NT, NR), jnp.float32)
    for depth_index in range(DEPTH):
        phases = vertical_waves * (depth_step * (depth_index + 1))
        cosine = jnp.cos(phases)
        sine_part = jnp.sin(phases)
        layer_real = spectrum[0, depth_index][None]
        layer_imag = spectrum[1, depth_index][None]
        pair_real = pair_real + (cosine * layer_real + sine_part * layer_imag)
        pair_imag = pair_imag + (cosine * layer_imag - sine_part * layer_real)
    field = jnp.fft.ifft2(lax.complex(pair_real, pair_imag), norm='ortho')
    tile_gate = jnp.repeat(jnp.repeat(aperture, TILE, axis=0), TILE, axis=1).astype(jnp.float32)
    weights = send_weight[:, None] * hear_weight[None, :] * tile_gate
    resid_real = weights[None] * (measured[0] - jnp.real(field))
    resid_imag = weights[None] * (measured[1] - jnp.imag(field))
    back = jnp.fft.fft2(lax.complex(resid_real, resid_imag), norm='ortho')
    back_real = jnp.real(back)
    back_imag = jnp.imag(back)
    layers_real = []
    layers_imag = []
    for depth_index in range(DEPTH):
        phases = vertical_waves * (depth_step * (depth_index + 1))
        cosine = jnp.cos(phases)
        sine_part = jnp.sin(phases)
        layers_real.append(lax.optimization_barrier(jnp.sum(cosine * back_real - sine_part * back_imag, axis=0)))
        layers_imag.append(lax.optimization_barrier(jnp.sum(cosine * back_imag + sine_part * back_real, axis=0)))
    gradient = jnp.stack([jnp.stack(layers_real), jnp.stack(layers_imag)])
    return (spectrum + step_size * gradient, jnp.stack([resid_real, resid_imag]))
```

```python
import functools
import math

import jax
import jax.numpy as jnp
from jax import lax
from jax.experimental import pallas as pl
from jax.experimental.pallas import tpu as pltpu
from jax.sharding import PartitionSpec as P


depth_step = 2.0
step_size = 0.125
root_floor = 0.25
radix = 4
limit = 60 << 20


def roots(wavenumber, offset, length, total):
    indices = offset + jnp.arange(length, dtype=jnp.int32)
    signed = jnp.where(indices < total // 2, indices, indices - total)
    waves = 2.0 * jnp.pi / total * signed.astype(jnp.float32)
    squared = (wavenumber * wavenumber)[:, None] - (waves * waves)[None, :]
    return jnp.sqrt(jnp.maximum(squared, 0.0) + root_floor)


def unit_pair(outer, inner, period):
    product = (
        jnp.arange(outer, dtype=jnp.int32)[:, None] * jnp.arange(inner, dtype=jnp.int32)[None, :] % period
    )
    phases = 2.0 * math.pi / period * product.astype(jnp.float32)
    return jnp.cos(phases), jnp.sin(phases)


def dft_tables(total):
    width = total // radix
    base_cos, base_sin = unit_pair(width, width, width)
    turn_cos, turn_sin = unit_pair(radix, width, total)
    scale = 1.0 / math.sqrt(total)
    turn_cos = turn_cos[:, None, :] * scale
    turn_sin = turn_sin[:, None, :] * scale
    return (
        turn_cos * base_cos - turn_sin * base_sin,
        turn_cos * base_sin + turn_sin * base_cos,
    )


def dft(pieces, tables, form, sign):
    (ar, ai), (br, bi), (cr, ci), (dr, di) = [(x[0], x[1]) for x in pieces]
    er, ei, gr, gi = ar + cr, ai + ci, ar - cr, ai - ci
    hr, hi, kr, ki = br + dr, bi + di, sign * (br - dr), sign * (bi - di)
    mixed_real = jnp.stack([er + hr, gr - ki, er - hr, gr + ki])
    mixed_imag = jnp.stack([ei + hi, gi + kr, ei - hi, gi - kr])
    mixed = jnp.stack([mixed_real, mixed_imag], axis=1)
    cosine, sine = tables
    first = jnp.einsum(form, cosine, mixed, precision=lax.Precision.HIGH)
    second = jnp.einsum(form, sine, mixed, precision=lax.Precision.HIGH)
    return jnp.stack(
        [
            first[:, :, 0] - sign * second[:, :, 1],
            first[:, :, 1] + sign * second[:, :, 0],
        ]
    )


def unmix(done, blocks):
    total = done.shape[1] * done.shape[2]
    rows = total // math.prod(blocks)
    freqs, width = done.shape[3:]
    done = jnp.transpose(done, (2, 1, 0, 3, 4)).reshape((math.prod(blocks), rows, 2, freqs, width))
    return jnp.transpose(done, (0, 2, 3, 1, 4)).reshape(tuple(blocks) + (2, freqs, rows, width))


def quarters(chunks, axis):
    count = chunks.shape[0]
    if count >= radix and count % radix == 0:
        step = count // radix
        return [
            jnp.concatenate([chunks[q * step + k] for k in range(step)], axis=axis) for q in range(radix)
        ]
    whole = jnp.concatenate([chunks[k] for k in range(count)], axis=axis)
    return jnp.split(whole, radix, axis=axis)


def exchange(values, axes):
    return lax.all_to_all(values, axes, split_axis=0, concat_axis=0, tiled=True)


def pair_kernel(layers, sent, heard, out):
    depth, rows = layers.shape[1:3]
    for f in range(out.shape[1]):
        hr = heard[0, f : f + 1, :]
        hi = heard[1, f : f + 1, :]
        for start in range(0, rows, 8):
            block = slice(start, start + 8)
            sr = sent[0, block, f : f + 1]
            si = sent[1, block, f : f + 1]
            zr = sr * hr - si * hi
            zi = -(sr * hi + si * hr)
            ar = layers[0, depth - 1, block, :]
            ai = layers[1, depth - 1, block, :]
            for j in range(depth - 1, -1, -1):
                ar, ai = ar * zr - ai * zi, ar * zi + ai * zr
                if j:
                    ar = ar + layers[0, j - 1, block, :]
                    ai = ai + layers[1, j - 1, block, :]
            out[0, f, block, :] = ar
            out[1, f, block, :] = ai


def gradient_kernel(pieces, sent, heard, out):
    freqs, rows = pieces.shape[1:3]
    depth = out.shape[1]
    for start in range(0, rows, 8):
        block = slice(start, start + 8)
        sums = [None] * depth
        for f in range(freqs):
            hr = heard[0, f : f + 1, :]
            hi = heard[1, f : f + 1, :]
            sr = sent[0, block, f : f + 1]
            si = sent[1, block, f : f + 1]
            zr = sr * hr - si * hi
            zi = sr * hi + si * hr
            tr = step_size * pieces[0, f, block, :]
            ti = step_size * pieces[1, f, block, :]
            for j in range(depth):
                tr, ti = tr * zr - ti * zi, tr * zi + ti * zr
                if f:
                    sums[j] = (sums[j][0] + tr, sums[j][1] + ti)
                else:
                    sums[j] = (tr, ti)
        for j in range(depth):
            out[0, j, block, :] = sums[j][0]
            out[1, j, block, :] = sums[j][1]


def pointwise(kernel, values, sent, heard, planes):
    _, count, rows, width = values.shape
    freqs = heard.shape[1]
    height = min(rows, 32)
    lanes = min(width, 128)
    return pl.pallas_call(
        kernel,
        grid=(rows // height, width // lanes),
        in_specs=[
            pl.BlockSpec((2, count, height, lanes), lambda i, k: (0, 0, i, k)),
            pl.BlockSpec((2, height, freqs), lambda i, k: (0, i, 0)),
            pl.BlockSpec((2, freqs, lanes), lambda i, k: (0, 0, k)),
        ],
        out_specs=pl.BlockSpec((2, planes, height, lanes), lambda i, k: (0, 0, i, k)),
        out_shape=jax.ShapeDtypeStruct((2, planes, rows, width), jnp.float32),
    )(values, sent, heard)


def per_device(spectrum, measured, wavenumber, send_weight, hear_weight, aperture):
    _, depth_local, rows_sent, rows_heard = spectrum.shape
    freq_local = measured.shape[1]
    freq_total = wavenumber.shape[0]
    senders = lax.axis_size("tx")
    hearers = lax.axis_size("rx")
    layers = lax.axis_size("freq")
    depth = depth_local * layers
    total_sent = rows_sent * senders
    total_heard = rows_heard * hearers
    slab = rows_sent // layers
    strip = rows_heard // senders
    band = rows_sent // hearers

    first_row = lax.axis_index("tx") * rows_sent + lax.axis_index("freq") * slab
    sent_phase = depth_step * roots(wavenumber, first_row, slab, total_sent).T
    heard_phase = depth_step * roots(wavenumber, lax.axis_index("rx") * rows_heard, rows_heard, total_heard)
    sent = jnp.stack([jnp.cos(sent_phase), jnp.sin(sent_phase)])
    heard = jnp.stack([jnp.cos(heard_phase), jnp.sin(heard_phase)])
    tables_sent = dft_tables(total_sent)
    tables_heard = tables_sent if total_heard == total_sent else dft_tables(total_heard)
    near = "qsm,qcfmw->qscfw"
    far = "qsm,qcfwm->qscfw"

    split = spectrum.reshape(2, depth_local, layers, slab, rows_heard)
    split = exchange(jnp.transpose(split, (2, 0, 1, 3, 4)), "freq")
    stacked = jnp.transpose(split, (1, 0, 2, 3, 4)).reshape(2, depth, slab, rows_heard)
    pair = pointwise(pair_kernel, stacked, sent, heard, freq_total)

    pair = pair.reshape(2, layers, freq_local, slab, senders, strip)
    pair = jnp.transpose(pair, (4, 1, 0, 2, 3, 5)).reshape(senders * layers, 2, freq_local, slab, strip)
    pair = exchange(pair, ("tx", "freq"))
    done = dft(quarters(pair, 2), tables_sent, near, 1.0)
    done = exchange(unmix(done, (senders * hearers,)), ("tx", "rx"))
    done = done.reshape((senders, hearers) + done.shape[1:])
    done = jnp.swapaxes(done, 0, 1).reshape((senders * hearers,) + done.shape[2:])
    done = dft(quarters(done, 3), tables_heard, far, 1.0)
    done = exchange(unmix(done, (hearers,)), "rx")
    field = jnp.transpose(done, (1, 2, 0, 4, 3)).reshape(2, freq_local, rows_sent, rows_heard)

    tiles_sent, tiles_heard = aperture.shape
    gate = aperture.astype(jnp.float32)
    weights = (
        send_weight.reshape(tiles_sent, -1)[:, :, None, None]
        * gate[:, None, :, None]
        * hear_weight.reshape(tiles_heard, -1)[None, None, :, :]
    ).reshape(rows_sent, rows_heard)
    residual = weights[None, None] * (measured - field)

    back = residual.reshape(2, freq_local, hearers, band, rows_heard)
    back = exchange(jnp.transpose(back, (2, 0, 1, 3, 4)), "rx")
    done = dft(quarters(back, 3), tables_heard, far, -1.0)
    done = unmix(done, (hearers, senders))
    done = jnp.swapaxes(done, 0, 1).reshape((senders * hearers,) + done.shape[2:])
    done = exchange(done, ("tx", "rx"))
    done = dft(quarters(done, 3), tables_sent, far, -1.0)
    done = exchange(unmix(done, (senders * layers,)), ("tx", "freq"))
    done = done.reshape(senders, layers, 2, freq_local, slab, strip)
    pieces = jnp.transpose(done, (2, 1, 3, 4, 0, 5)).reshape(2, freq_total, slab, rows_heard)

    gradient = pointwise(gradient_kernel, pieces, sent, heard, depth)
    gradient = gradient.reshape(2, layers, depth_local, slab, rows_heard)
    gradient = exchange(jnp.transpose(gradient, (1, 0, 2, 3, 4)), "freq")
    gradient = jnp.transpose(gradient, (1, 2, 0, 3, 4)).reshape(spectrum.shape)
    return (spectrum + gradient, residual)


lanes = 128
chunks = 2


def split(values):
    high = values.astype(jnp.bfloat16)
    return high, (values - high.astype(jnp.float32)).astype(jnp.bfloat16)


def split_table(values):
    high = lax.reduce_precision(values, 8, 7)
    return high.astype(jnp.bfloat16), (values - high).astype(jnp.bfloat16)


def stacked_tables(total):
    width = total // radix
    base = unit_pair(width, width, width)
    turn = unit_pair(radix, width, total)
    scale = 1.0 / math.sqrt(total)
    forms = []
    for where in ((slice(None), None, slice(None)), (slice(None), slice(None), None)):
        turn_cos, turn_sin = turn[0][where] * scale, turn[1][where] * scale
        cosine = turn_cos * base[0] - turn_sin * base[1]
        sine = turn_cos * base[1] + turn_sin * base[0]
        forms.append(jnp.stack(split_table(cosine) + split_table(sine), axis=1))
    return forms


def turned(table, s, high, low, left):
    def times(values, kind):
        pair = (table[s, kind], values) if left else (values, table[s, kind])
        return jnp.dot(*pair, preferred_element_type=jnp.float32)

    first = times(high, 0) + (times(high, 1) + times(low, 0))
    second = times(high, 2) + (times(high, 3) + times(low, 2))
    return first, second


def mix(parts, sign):
    (ar, ai), (br, bi), (cr, ci), (dr, di) = parts
    er, ei, gr, gi = ar + cr, ai + ci, ar - cr, ai - ci
    hr, hi, kr, ki = br + dr, bi + di, sign * (br - dr), sign * (bi - di)
    return (er + hr, ei + hi), (gr - ki, gi + kr), (er - hr, ei - hi), (gr + ki, gi - kr)


def aligned(index, size):
    return pl.ds(pl.multiple_of(index * size, size), size)


def phase_of(sent, heard, f, rows, columns):
    hr, hi = heard[0, f : f + 1, columns], heard[1, f : f + 1, columns]
    sr, si = sent[0, rows, f : f + 1], sent[1, rows, f : f + 1]
    return sr * hr - si * hi, sr * hi + si * hr


def pair_rows_kernel(local, step, layers, sent, heard, table, *rest):
    out, high, low = rest[-3:]
    hearers, groups, _, per, rows, width = layers.shape
    senders, part = out.shape[0], width // hearers
    turns = radix // senders
    spans = width // lanes
    block = groups * rows
    for g in range(groups):
        f = g * local + step

        def body(t, carry):
            row, span = t // spans, t % spans
            down, across = aligned(row, 16), aligned(span, lanes)
            parts = []
            for h in range(hearers):
                zr, zi = phase_of(sent, heard, f, down, aligned(h * spans + span, lanes))
                ar = layers[h, groups - 1, 0, per - 1, down, across]
                ai = layers[h, groups - 1, 1, per - 1, down, across]
                for j in range(groups * per - 1, -1, -1):
                    ar, ai = ar * zr + ai * zi, ai * zr - ar * zi
                    if j:
                        q, d = divmod(j - 1, per)
                        ar = ar + layers[h, q, 0, d, down, across]
                        ai = ai + layers[h, q, 1, d, down, across]
                parts.append((ar, ai))
            for s, values in enumerate(mix(parts, 1.0)):
                for c in range(2):
                    place = aligned((c * block + g * rows) // 16 + row, 16)
                    high[s, place, across], low[s, place, across] = split(values[c])
            return carry

        lax.fori_loop(0, rows // 16 * spans, body, 0)
    for s in range(radix):
        first, second = turned(table, s, high[s], low[s], False)
        real = first[:block] - second[block:]
        imag = first[block:] + second[:block]
        columns = slice(s % turns * part, (s % turns + 1) * part)
        for g in range(groups):
            for p in range(hearers):
                piece = (slice(g * rows, (g + 1) * rows), slice(p * part, (p + 1) * part))
                out[s // turns, p, g, 0, :, columns] = real[piece]
                out[s // turns, p, g, 1, :, columns] = imag[piece]


def pair_rows(layers, sent, heard, table, local, step, senders, before, count, chunk):
    hearers, groups, _, per, rows, width = layers.shape
    height = min(rows, 32)
    strip = width // senders
    freqs = groups * local
    first = chunk * (rows // height)
    return pl.pallas_call(
        functools.partial(pair_rows_kernel, local, step),
        grid=(rows // height,),
        in_specs=[
            pl.BlockSpec((hearers, groups, 2, per, height, width), lambda i: (0, 0, 0, 0, i, 0)),
            pl.BlockSpec((2, height, freqs), lambda i: (0, i, 0)),
            pl.BlockSpec((2, freqs, hearers * width), lambda i: (0, 0, 0)),
            pl.BlockSpec(table.shape, lambda i: (0, 0, 0, 0), pipeline_mode=pl.Buffered(1)),
        ]
        + [pl.BlockSpec(memory_space=pl.ANY)] * (before is not None),
        out_specs=pl.BlockSpec(
            (senders, hearers, groups, 2, height, strip), lambda i: (0, 0, 0, 0, i + first, 0)
        ),
        out_shape=jax.ShapeDtypeStruct((senders, hearers, groups, 2, rows * count, strip), jnp.float32),
        scratch_shapes=[pltpu.VMEM((radix, 2 * groups * height, width), jnp.bfloat16)] * 2,
        input_output_aliases={} if before is None else {4: 0},
        compiler_params=pltpu.CompilerParams(vmem_limit_bytes=limit),
        cost_estimate=pl.CostEstimate(flops=6 * 10**9, bytes_accessed=24 << 20, transcendentals=0),
    )(layers, sent, heard, table, *([] if before is None else [before]))


def gradient_rows_kernel(local, step, pieces, sent, heard, table, *rest):
    before = rest[0] if len(rest) == 5 else None
    out, high, low, done = rest[-4:]
    senders, hearers, groups, _, rows, _ = pieces.shape
    width, per = out.shape[5], out.shape[3]
    part = width // hearers
    turns = radix // senders
    spans = width // lanes
    block = groups * rows
    for s in range(radix):
        columns = slice(s % turns * part, (s % turns + 1) * part)
        for g in range(groups):
            for c in range(2):
                down = slice(c * block + g * rows, c * block + (g + 1) * rows)
                for p in range(hearers):
                    across = slice(p * part, (p + 1) * part)
                    values = pieces[s // turns, p, g, c, :, columns]
                    high[s, down, across], low[s, down, across] = split(values)
    for s in range(radix):
        first, second = turned(table, s, high[s], low[s], False)
        done[s, 0] = first[:block] + second[block:]
        done[s, 1] = first[block:] - second[:block]

    def body(t, carry):
        row, span = t // spans, t % spans
        across = aligned(span, lanes)
        for g in range(groups):
            down = aligned(g * rows // 8 + row, 8)
            parts = [(done[s, 0, down, across], done[s, 1, down, across]) for s in range(radix)]
            for h, (real, imag) in enumerate(mix(parts, -1.0)):
                done[h, 0, down, across] = step_size * real
                done[h, 1, down, across] = step_size * imag
        here = aligned(row, 8)
        for h in range(hearers):
            sums = [None] * (groups * per)
            for g in range(groups):
                zr, zi = phase_of(sent, heard, g * local + step, here, aligned(h * spans + span, lanes))
                down = aligned(g * rows // 8 + row, 8)
                tr, ti = done[h, 0, down, across], done[h, 1, down, across]
                for j in range(groups * per):
                    tr, ti = tr * zr - ti * zi, tr * zi + ti * zr
                    sums[j] = (sums[j][0] + tr, sums[j][1] + ti) if g else (tr, ti)
            for j in range(groups * per):
                q, d = divmod(j, per)
                for c in range(2):
                    value = sums[j][c]
                    if before is not None:
                        value = value + before[h, q, c, d, here, across]
                    out[h, q, c, d, here, across] = value
        return carry

    lax.fori_loop(0, rows // 8 * spans, body, 0)


def gradient_rows(pieces, sent, heard, table, before, local, step, per, chunk):
    senders, hearers, groups, _, _, strip = pieces.shape
    rows = sent.shape[1]
    width = strip * senders
    height = min(rows, 32)
    first = chunk * (rows // height)
    freqs = groups * local
    cube = pl.BlockSpec((hearers, groups, 2, per, height, width), lambda i: (0, 0, 0, 0, i, 0))
    return pl.pallas_call(
        functools.partial(gradient_rows_kernel, local, step),
        grid=(rows // height,),
        in_specs=[
            pl.BlockSpec((senders, hearers, groups, 2, height, strip), lambda i: (0, 0, 0, 0, i + first, 0)),
            pl.BlockSpec((2, height, freqs), lambda i: (0, i, 0)),
            pl.BlockSpec((2, freqs, hearers * width), lambda i: (0, 0, 0)),
            pl.BlockSpec(table.shape, lambda i: (0, 0, 0, 0), pipeline_mode=pl.Buffered(1)),
        ]
        + [cube] * (before is not None),
        out_specs=cube,
        out_shape=jax.ShapeDtypeStruct((hearers, groups, 2, per, rows, width), jnp.float32),
        scratch_shapes=[pltpu.VMEM((radix, 2 * groups * height, width), jnp.bfloat16)] * 2
        + [pltpu.VMEM((radix, 2, groups * height, width), jnp.float32)],
        compiler_params=pltpu.CompilerParams(vmem_limit_bytes=limit),
        cost_estimate=pl.CostEstimate(flops=6 * 10**9, bytes_accessed=24 << 20, transcendentals=0),
    )(pieces, sent, heard, table, *([] if before is None else [before]))


def columns_kernel(count, parts_out, senders, place, *refs):
    ins, refs = refs[:count], refs[count:]
    seen, refs = refs[:senders], refs[senders:]
    weights, refs = refs[:senders], refs[senders:]
    ahead, behind, refs = refs[0], refs[1], refs[2:]
    outs, refs = refs[:parts_out], refs[parts_out:]
    left, refs = refs[:senders], refs[senders:]
    high, low, field = refs
    devices, _, rows, _ = ins[0].shape
    groups = devices // radix
    width = high.shape[1]
    rest = width // senders
    me = place[0]

    def gather(d, carry):
        for n in range(count):
            parts = [(ins[n][q * groups + d, 0], ins[n][q * groups + d, 1]) for q in range(radix)]
            down = aligned(d * count + n, rows)
            for s, values in enumerate(mix(parts, 1.0)):
                for c in range(2):
                    across = slice(c * lanes, (c + 1) * lanes)
                    high[s, down, across], low[s, down, across] = split(values[c])
        return carry

    lax.fori_loop(0, groups, gather, 0)
    for s in range(radix):
        first, second = turned(ahead, s, high[s], low[s], True)
        field[s, :, :lanes] = first[:, :lanes] - second[:, lanes:]
        field[s, :, lanes:] = first[:, lanes:] + second[:, :lanes]
        for shift in range(senders):
            down = aligned(lax.rem(me + senders - shift, senders), rest)
            weight = weights[shift][0, s]
            for c in range(2):
                across = slice(c * lanes, (c + 1) * lanes)
                values = weight * (seen[shift][c, s] - field[s, down, across])
                left[shift][c, s] = values
                high[s, down, across], low[s, down, across] = split(values)
    for s in range(radix):
        first, second = turned(behind, s, high[s], low[s], True)
        field[s, :, :lanes] = first[:, :lanes] + second[:, lanes:]
        field[s, :, lanes:] = first[:, lanes:] - second[:, :lanes]

    def scatter(d, carry):
        for n in range(parts_out):
            down = aligned(d * parts_out + n, rows * count // parts_out)
            parts = [(field[s, down, :lanes], field[s, down, lanes:]) for s in range(radix)]
            for q, values in enumerate(mix(parts, -1.0)):
                for c in range(2):
                    outs[n][q * groups + d, c] = values[c]
        return carry

    lax.fori_loop(0, groups, scatter, 0)


def columns(pieces, seen, ahead, behind, step, place, parts_out):
    count, senders = len(pieces), len(seen)
    devices, _, rows, strip = pieces[0].shape
    planes, _, rest, _ = seen[0].shape
    width = rest * senders
    moved = pl.BlockSpec((devices, 2, rows, lanes), lambda i, place: (0, 0, 0, i))
    short = rows * count // parts_out
    sent_on = pl.BlockSpec((devices, 2, short, lanes), lambda i, place: (0, 0, 0, i))
    table = pl.BlockSpec(ahead.shape, lambda i, place: (0, 0, 0, 0), pipeline_mode=pl.Buffered(1))
    outs = pl.pallas_call(
        functools.partial(columns_kernel, count, parts_out, senders),
        grid_spec=pltpu.PrefetchScalarGridSpec(
            num_scalar_prefetch=1,
            grid=(strip // lanes,),
            in_specs=[moved] * count
            + [pl.BlockSpec((2, radix, rest, lanes), lambda i, place: (step, 0, 0, i))] * senders
            + [pl.BlockSpec((1, radix, rest, lanes), lambda i, place: (planes - 1, 0, 0, i))] * senders
            + [table, table],
            out_specs=[sent_on] * parts_out
            + [pl.BlockSpec((2, radix, rest, lanes), lambda i, place: (0, 0, 0, i))] * senders,
            scratch_shapes=[pltpu.VMEM((radix, width, 2 * lanes), jnp.bfloat16)] * 2
            + [pltpu.VMEM((radix, width, 2 * lanes), jnp.float32)],
        ),
        out_shape=[jax.ShapeDtypeStruct((devices, 2, short, strip), jnp.float32)] * parts_out
        + [jax.ShapeDtypeStruct((2, radix, rest, strip), jnp.float32)] * senders,
        compiler_params=pltpu.CompilerParams(vmem_limit_bytes=limit),
        cost_estimate=pl.CostEstimate(flops=12 * 10**9, bytes_accessed=36 << 20, transcendentals=0),
    )(place, *pieces, *seen, *[x for x in seen], ahead, behind)
    return outs[:parts_out], outs[parts_out:]


def moved_exactly(values, table):
    high = values.astype(jnp.bfloat16)
    rest = values - high.astype(jnp.float32)
    middle = rest.astype(jnp.bfloat16)
    low = (rest - middle.astype(jnp.float32)).astype(jnp.bfloat16)
    first, second, third = [jnp.dot(x, table, preferred_element_type=jnp.float32) for x in (high, middle, low)]
    return (first + second) + third


def spread_kernel(senders, place, measured, send, hear, gate, table, *outs):
    outs, held = outs[:-1], outs[-1]
    _, local, rows, width = measured.shape
    strip = width // senders
    part = width // radix
    turns = radix // senders
    tall = rows // radix
    me = place[0]
    spans = [slice(k * lanes, (k + 1) * lanes) for k in range(width // lanes)]
    for f in range(local):
        for c in range(2):
            for k, across in enumerate(spans):
                held[k] = measured[c, f, :, across]
            for s in range(radix):
                picked = pl.ds(s, tall, stride=radix)
                values = jnp.concatenate([held[k, picked, :] for k in range(len(spans))], axis=1)
                for shift in range(senders):
                    target = lax.rem(me + shift, senders)
                    outs[shift][2 * f + c, s] = moved_exactly(values, table[:, aligned(target, strip)])
    for shift in range(senders):
        target = lax.rem(me + shift, senders)
        for s in range(radix):
            for n in range(turns):
                across = slice(n * part, (n + 1) * part)
                outer = send[s] * hear[target * turns + n]
                outs[shift][2 * local, s, :, across] = outer * gate[...]


def spread(measured, send, hear, gate, table, place, senders):
    _, local, rows, width = measured.shape
    height = min(rows, 256)
    strip = width // senders
    rest, tall = rows // radix, height // radix
    part = width // radix
    return pl.pallas_call(
        functools.partial(spread_kernel, senders),
        grid_spec=pltpu.PrefetchScalarGridSpec(
            num_scalar_prefetch=1,
            grid=(rows // height,),
            in_specs=[
                pl.BlockSpec((2, local, height, width), lambda i, place: (0, 0, i, 0)),
                pl.BlockSpec((radix, tall, 1), lambda i, place: (0, i, 0)),
                pl.BlockSpec((radix, 1, part), lambda i, place: (0, 0, 0)),
                pl.BlockSpec((tall, part), lambda i, place: (i, 0)),
                pl.BlockSpec((width, width), lambda i, place: (0, 0)),
            ],
            out_specs=[pl.BlockSpec((2 * local + 1, radix, tall, strip), lambda i, place: (0, 0, i, 0))] * senders,
            scratch_shapes=[pltpu.VMEM((width // lanes, height, lanes), jnp.float32)],
        ),
        out_shape=[jax.ShapeDtypeStruct((2 * local + 1, radix, rest, strip), jnp.float32)] * senders,
        compiler_params=pltpu.CompilerParams(vmem_limit_bytes=limit),
        cost_estimate=pl.CostEstimate(flops=6 * 10**9, bytes_accessed=18 << 20, transcendentals=0),
    )(place, measured, send, hear, gate, table)


def join_kernel(local, senders, place, *refs):
    ins, table, out, held = refs[: local * senders], refs[-3], refs[-2], refs[-1]
    tall, strip = ins[0].shape[2:]
    spans = [slice(k * lanes, (k + 1) * lanes) for k in range(strip * senders // lanes)]
    me = place[0]
    for f in range(local):
        for c in range(2):
            for s in range(radix):
                total = None
                for shift in range(senders):
                    source = lax.rem(me + shift, senders)
                    moved = moved_exactly(ins[f * senders + shift][c, s], table[aligned(source, strip), :])
                    total = moved if total is None else total + moved
                for k, across in enumerate(spans):
                    held[k, pl.ds(s, tall, stride=radix), :] = total[:, across]
            for k, across in enumerate(spans):
                out[c, f, :, across] = held[k]


def join(pieces, table, place):
    local, senders = len(pieces), len(pieces[0])
    _, _, rest, strip = pieces[0][0].shape
    rows, width = rest * radix, strip * senders
    height = min(rows, 256)
    return pl.pallas_call(
        functools.partial(join_kernel, local, senders),
        grid_spec=pltpu.PrefetchScalarGridSpec(
            num_scalar_prefetch=1,
            grid=(rows // height,),
            in_specs=[pl.BlockSpec((2, radix, height // radix, strip), lambda i, place: (0, 0, i, 0))]
            * (local * senders)
            + [pl.BlockSpec((width, width), lambda i, place: (0, 0))],
            out_specs=pl.BlockSpec((2, local, height, width), lambda i, place: (0, 0, i, 0)),
            scratch_shapes=[pltpu.VMEM((width // lanes, height, lanes), jnp.float32)],
        ),
        out_shape=jax.ShapeDtypeStruct((2, local, rows, width), jnp.float32),
        compiler_params=pltpu.CompilerParams(vmem_limit_bytes=limit),
        cost_estimate=pl.CostEstimate(flops=6 * 10**9, bytes_accessed=16 << 20, transcendentals=0),
    )(place, *[x for group in pieces for x in group], table)


def add_kernel(spectrum, moved, *rest):
    for k in range(moved.shape[0]):
        rest[-1][:, :, k, 0] = spectrum[:, :, k, 0] + moved[k]


def add(spectrum, moved, before, chunk):
    groups, _, per, rows, width = moved.shape
    count = spectrum.shape[2] // (groups * rows)
    spectrum = spectrum.reshape(2, per, groups, count, rows, width)
    some = math.gcd(groups, 2)
    block = pl.BlockSpec((2, per, some, 1, rows, width), lambda i: (0, 0, i, chunk, 0, 0))
    return pl.pallas_call(
        add_kernel,
        grid=(groups // some,),
        in_specs=[block, pl.BlockSpec((some, 2, per, rows, width), lambda i: (i, 0, 0, 0, 0))]
        + [pl.BlockSpec(memory_space=pl.ANY)] * (before is not None),
        out_specs=block,
        out_shape=jax.ShapeDtypeStruct(spectrum.shape, jnp.float32),
        input_output_aliases={} if before is None else {2: 0},
        cost_estimate=pl.CostEstimate(flops=2 * 10**6, bytes_accessed=12 << 20, transcendentals=0),
    )(spectrum, moved, *([] if before is None else [before]))


def passed(values, axis, way):
    count = lax.axis_size(axis)
    return [values[0]] + [
        lax.ppermute(values[shift], axis, [(k, (k + way * shift) % count) for k in range(count)])
        for shift in range(1, count)
    ]


def per_device_tiled(spectrum, measured, wavenumber, send_weight, hear_weight, aperture):
    _, per, rows_sent, rows_heard = spectrum.shape
    local = measured.shape[1]
    senders = lax.axis_size("tx")
    hearers = lax.axis_size("rx")
    layers = lax.axis_size("freq")
    total_sent = rows_sent * senders
    total_heard = rows_heard * hearers
    groups = hearers * layers
    slab = rows_sent // groups
    rows = slab // chunks
    place = lax.axis_index("tx").reshape(1).astype(jnp.int32)

    first_row = lax.axis_index("tx") * rows_sent + (lax.axis_index("rx") * layers + lax.axis_index("freq")) * slab
    sent_phase = depth_step * roots(wavenumber, first_row, slab, total_sent).T
    heard_phase = depth_step * roots(wavenumber, 0, total_heard, total_heard)
    sent = jnp.stack([jnp.cos(sent_phase), jnp.sin(sent_phase)])
    heard = jnp.stack([jnp.cos(heard_phase), jnp.sin(heard_phase)])
    sents = [sent[:, n * rows : (n + 1) * rows] for n in range(chunks)]
    ahead_sent, behind_sent = stacked_tables(total_sent)
    ahead_heard, behind_heard = (
        (ahead_sent, behind_sent) if total_heard == total_sent else stacked_tables(total_heard)
    )

    order = jnp.arange(rows_heard, dtype=jnp.int32)
    order = order % (rows_heard // radix) * radix + order // (rows_heard // radix)
    picks = (jnp.arange(rows_heard, dtype=jnp.int32)[:, None] == order[None, :]).astype(jnp.bfloat16)
    tile_sent = rows_sent // aperture.shape[0] // radix
    tile_heard = rows_heard // aperture.shape[1] // radix
    gate = jnp.repeat(jnp.repeat(aperture, tile_sent, axis=0), tile_heard, axis=1).astype(jnp.float32)
    send = send_weight.reshape(-1, radix).T[:, :, None]
    hear = hear_weight.reshape(-1, radix).T[:, None, :]

    everyone = ("tx", "rx", "freq")
    cube = (hearers, layers, 2, per, rows, rows_heard)

    def flat(x):
        return x.reshape((senders * hearers * layers,) + x.shape[3:])

    def boxed(x):
        return x.reshape((senders, hearers, layers) + x.shape[1:])

    blocks = spectrum.reshape(2, per, groups, chunks, rows, rows_heard)
    arrived = []
    for n in range(chunks):
        block = jnp.transpose(blocks[:, :, :, n], (2, 0, 1, 3, 4))
        arrived.append(exchange(block, ("rx", "freq")).reshape(cube))
    seen = spread(measured, send, hear, gate, picks, place, senders)
    seen = passed(seen, "tx", 1)

    def pair_of(f, n, before, count):
        where = n if count > 1 else 0
        return pair_rows(
            arrived[n], sents[n], heard, behind_heard, local, f, senders, before, count, where
        )

    pairs = []
    for f in range(local):
        if f == 0:
            made = [pair_of(f, n, None, 1) for n in range(chunks)]
        else:
            whole = None
            for n in range(chunks):
                whole = pair_of(f, n, whole, chunks)
            made = [whole]
        moved = []
        for x in made:
            moved.append(exchange(flat(x), everyone))
        pairs.append(moved)
    residuals = []
    gradient = [None] * chunks
    for f in range(local):
        count = chunks if f == local - 1 else 1
        backs, left = columns(pairs[f], seen, ahead_sent, behind_sent, f, place, count)
        residuals.append(passed(left, "tx", -1))
        moved = []
        for n in range(count):
            moved.append(boxed(exchange(backs[n], everyone)))
        for n in range(chunks):
            pieces, where = (moved[n], 0) if count > 1 else (moved[0], n)
            gradient[n] = gradient_rows(
                pieces, sents[n], heard, ahead_heard, gradient[n], local, f, per, where
            )
    updated = None
    moved = []
    for n in range(chunks):
        flat_gradient = gradient[n].reshape(groups, 2, per, rows, rows_heard)
        moved.append(exchange(flat_gradient, ("rx", "freq")))
    for n in range(chunks):
        updated = add(spectrum, moved[n], updated, n)
    residual = join(residuals, picks.T, place)
    return (updated.reshape(spectrum.shape), residual)


def fits(mesh, sent, heard):
    senders, hearers, layers = [mesh.shape[axis] for axis in ("tx", "rx", "freq")]
    rows = sent // senders // (hearers * layers)
    return (
        hearers == radix
        and radix % senders == 0
        and rows % (32 * chunks) == 0
        and heard // hearers // radix % lanes == 0
        and sent // senders % 256 == 0
    )


def solution(mesh):
    placed = (
        P(None, "freq", "tx", "rx"),
        P(None, "freq", "tx", "rx"),
        P(),
        P("tx"),
        P("rx"),
        P("tx", "rx"),
    )

    def body(*args):
        sent, heard = args[3].shape[0] * mesh.shape["tx"], args[4].shape[0] * mesh.shape["rx"]
        local = args[1].shape[1]
        return (per_device_tiled if fits(mesh, sent, heard) and local == 2 else per_device)(*args)

    return jax.shard_map(
        body,
        mesh=mesh,
        in_specs=placed,
        out_specs=(P(None, "freq", "tx", "rx"), P(None, "freq", "tx", "rx")),
        check_vma=False,
    )
```

```python
import math

import jax
import jax.numpy as jnp
from jax import lax
from jax.experimental import pallas as pl
from jax.experimental.pallas import tpu as pltpu
from jax.sharding import PartitionSpec as P

depth_step = 2.0
step_size = 0.125
root_floor = 0.25
radix = 4
limit = 67043328


def roots(wavenumber, offset, length, total):
    indices = offset + jnp.arange(length, dtype=jnp.int32)
    signed = jnp.where(indices < total // 2, indices, indices - total)
    waves = 2.0 * jnp.pi / total * signed.astype(jnp.float32)
    squared = (wavenumber * wavenumber)[:, None] - (waves * waves)[None, :]
    return jnp.sqrt(jnp.maximum(squared, 0.0) + root_floor)


def unit_pair(outer, inner, period):
    product = (
        jnp.arange(outer, dtype=jnp.int32)[:, None] * jnp.arange(inner, dtype=jnp.int32)[None, :] % period
    )
    phases = 2.0 * math.pi / period * product.astype(jnp.float32)
    return jnp.cos(phases), jnp.sin(phases)


def dft_tables(total):
    width = total // radix
    base_cos, base_sin = unit_pair(width, width, width)
    turn_cos, turn_sin = unit_pair(radix, width, total)
    scale = 1.0 / math.sqrt(total)
    turn_cos = turn_cos[:, None, :] * scale
    turn_sin = turn_sin[:, None, :] * scale
    return (
        turn_cos * base_cos - turn_sin * base_sin,
        turn_cos * base_sin + turn_sin * base_cos,
    )


def dft(pieces, tables, form, sign):
    (ar, ai), (br, bi), (cr, ci), (dr, di) = [(x[0], x[1]) for x in pieces]
    er, ei, gr, gi = ar + cr, ai + ci, ar - cr, ai - ci
    hr, hi, kr, ki = br + dr, bi + di, sign * (br - dr), sign * (bi - di)
    mixed_real = jnp.stack([er + hr, gr - ki, er - hr, gr + ki])
    mixed_imag = jnp.stack([ei + hi, gi + kr, ei - hi, gi - kr])
    mixed = jnp.stack([mixed_real, mixed_imag], axis=1)
    cosine, sine = tables
    first = jnp.einsum(form, cosine, mixed, precision=lax.Precision.HIGH)
    second = jnp.einsum(form, sine, mixed, precision=lax.Precision.HIGH)
    return jnp.stack(
        [
            first[:, :, 0] - sign * second[:, :, 1],
            first[:, :, 1] + sign * second[:, :, 0],
        ]
    )


def unmix(done, blocks):
    total = done.shape[1] * done.shape[2]
    rows = total // math.prod(blocks)
    freqs, width = done.shape[3:]
    done = jnp.transpose(done, (2, 1, 0, 3, 4)).reshape((math.prod(blocks), rows, 2, freqs, width))
    return jnp.transpose(done, (0, 2, 3, 1, 4)).reshape(tuple(blocks) + (2, freqs, rows, width))


def quarters(chunks, axis):
    count = chunks.shape[0]
    if count >= radix and count % radix == 0:
        step = count // radix
        return [
            jnp.concatenate([chunks[q * step + k] for k in range(step)], axis=axis) for q in range(radix)
        ]
    whole = jnp.concatenate([chunks[k] for k in range(count)], axis=axis)
    return jnp.split(whole, radix, axis=axis)


def exchange(values, axes):
    return lax.all_to_all(values, axes, split_axis=0, concat_axis=0, tiled=True)


def pair_kernel(layers, sent, heard, out):
    depth, rows = layers.shape[1:3]
    for f in range(out.shape[1]):
        hr = heard[0, f : f + 1, :]
        hi = heard[1, f : f + 1, :]
        for start in range(0, rows, 8):
            block = slice(start, start + 8)
            sr = sent[0, block, f : f + 1]
            si = sent[1, block, f : f + 1]
            zr = sr * hr - si * hi
            zi = -(sr * hi + si * hr)
            ar = layers[0, depth - 1, block, :]
            ai = layers[1, depth - 1, block, :]
            for j in range(depth - 1, -1, -1):
                ar, ai = ar * zr - ai * zi, ar * zi + ai * zr
                if j:
                    ar = ar + layers[0, j - 1, block, :]
                    ai = ai + layers[1, j - 1, block, :]
            out[0, f, block, :] = ar
            out[1, f, block, :] = ai


def gradient_kernel(pieces, sent, heard, out):
    freqs, rows = pieces.shape[1:3]
    depth = out.shape[1]
    for start in range(0, rows, 8):
        block = slice(start, start + 8)
        sums = [None] * depth
        for f in range(freqs):
            hr = heard[0, f : f + 1, :]
            hi = heard[1, f : f + 1, :]
            sr = sent[0, block, f : f + 1]
            si = sent[1, block, f : f + 1]
            zr = sr * hr - si * hi
            zi = sr * hi + si * hr
            tr = step_size * pieces[0, f, block, :]
            ti = step_size * pieces[1, f, block, :]
            for j in range(depth):
                tr, ti = tr * zr - ti * zi, tr * zi + ti * zr
                if f:
                    sums[j] = (sums[j][0] + tr, sums[j][1] + ti)
                else:
                    sums[j] = (tr, ti)
        for j in range(depth):
            out[0, j, block, :] = sums[j][0]
            out[1, j, block, :] = sums[j][1]


def pointwise(kernel, values, sent, heard, planes):
    _, count, rows, width = values.shape
    freqs = heard.shape[1]
    height = min(rows, 32)
    lanes = min(width, 128)
    return pl.pallas_call(
        kernel,
        grid=(rows // height, width // lanes),
        in_specs=[
            pl.BlockSpec((2, count, height, lanes), lambda i, k: (0, 0, i, k)),
            pl.BlockSpec((2, height, freqs), lambda i, k: (0, i, 0)),
            pl.BlockSpec((2, freqs, lanes), lambda i, k: (0, 0, k)),
        ],
        out_specs=pl.BlockSpec((2, planes, height, lanes), lambda i, k: (0, 0, i, k)),
        out_shape=jax.ShapeDtypeStruct((2, planes, rows, width), jnp.float32),
    )(values, sent, heard)


def per_device(spectrum, measured, wavenumber, send_weight, hear_weight, aperture):
    _, depth_local, rows_sent, rows_heard = spectrum.shape
    freq_local = measured.shape[1]
    freq_total = wavenumber.shape[0]
    senders = lax.axis_size("tx")
    hearers = lax.axis_size("rx")
    layers = lax.axis_size("freq")
    depth = depth_local * layers
    total_sent = rows_sent * senders
    total_heard = rows_heard * hearers
    slab = rows_sent // layers
    strip = rows_heard // senders
    band = rows_sent // hearers

    first_row = lax.axis_index("tx") * rows_sent + lax.axis_index("freq") * slab
    sent_phase = depth_step * roots(wavenumber, first_row, slab, total_sent).T
    heard_phase = depth_step * roots(wavenumber, lax.axis_index("rx") * rows_heard, rows_heard, total_heard)
    sent = jnp.stack([jnp.cos(sent_phase), jnp.sin(sent_phase)])
    heard = jnp.stack([jnp.cos(heard_phase), jnp.sin(heard_phase)])
    tables_sent = dft_tables(total_sent)
    tables_heard = tables_sent if total_heard == total_sent else dft_tables(total_heard)
    near = "qsm,qcfmw->qscfw"
    far = "qsm,qcfwm->qscfw"

    split = spectrum.reshape(2, depth_local, layers, slab, rows_heard)
    split = exchange(jnp.transpose(split, (2, 0, 1, 3, 4)), "freq")
    stacked = jnp.transpose(split, (1, 0, 2, 3, 4)).reshape(2, depth, slab, rows_heard)
    pair = pointwise(pair_kernel, stacked, sent, heard, freq_total)

    pair = pair.reshape(2, layers, freq_local, slab, senders, strip)
    pair = jnp.transpose(pair, (4, 1, 0, 2, 3, 5)).reshape(senders * layers, 2, freq_local, slab, strip)
    pair = exchange(pair, ("tx", "freq"))
    done = dft(quarters(pair, 2), tables_sent, near, 1.0)
    done = exchange(unmix(done, (senders * hearers,)), ("tx", "rx"))
    done = done.reshape((senders, hearers) + done.shape[1:])
    done = jnp.swapaxes(done, 0, 1).reshape((senders * hearers,) + done.shape[2:])
    done = dft(quarters(done, 3), tables_heard, far, 1.0)
    done = exchange(unmix(done, (hearers,)), "rx")
    field = jnp.transpose(done, (1, 2, 0, 4, 3)).reshape(2, freq_local, rows_sent, rows_heard)

    tiles_sent, tiles_heard = aperture.shape
    gate = aperture.astype(jnp.float32)
    weights = (
        send_weight.reshape(tiles_sent, -1)[:, :, None, None]
        * gate[:, None, :, None]
        * hear_weight.reshape(tiles_heard, -1)[None, None, :, :]
    ).reshape(rows_sent, rows_heard)
    residual = weights[None, None] * (measured - field)

    back = residual.reshape(2, freq_local, hearers, band, rows_heard)
    back = exchange(jnp.transpose(back, (2, 0, 1, 3, 4)), "rx")
    done = dft(quarters(back, 3), tables_heard, far, -1.0)
    done = unmix(done, (hearers, senders))
    done = jnp.swapaxes(done, 0, 1).reshape((senders * hearers,) + done.shape[2:])
    done = exchange(done, ("tx", "rx"))
    done = dft(quarters(done, 3), tables_sent, far, -1.0)
    done = exchange(unmix(done, (senders * layers,)), ("tx", "freq"))
    done = done.reshape(senders, layers, 2, freq_local, slab, strip)
    pieces = jnp.transpose(done, (2, 1, 3, 4, 0, 5)).reshape(2, freq_total, slab, rows_heard)

    gradient = pointwise(gradient_kernel, pieces, sent, heard, depth)
    gradient = gradient.reshape(2, layers, depth_local, slab, rows_heard)
    gradient = exchange(jnp.transpose(gradient, (1, 0, 2, 3, 4)), "freq")
    gradient = jnp.transpose(gradient, (1, 2, 0, 3, 4)).reshape(spectrum.shape)
    return (spectrum + gradient, residual)


lanes = 128
chunks = 2
mesh_ids = pl.DeviceIdType.MESH


def split(values):
    high = values.astype(jnp.bfloat16)
    return high, (values - high.astype(jnp.float32)).astype(jnp.bfloat16)


def split_table(values):
    high = lax.reduce_precision(values, 8, 7)
    return high.astype(jnp.bfloat16), (values - high).astype(jnp.bfloat16)


def multiply(left, right):
    return jnp.dot(left, right, preferred_element_type=jnp.float32)


def turned(base, high, low, left):
    def times(values, kind):
        return multiply(base[kind], values) if left else multiply(values, base[kind])

    first = times(high, 0) + (times(high, 1) + times(low, 0))
    second = times(high, 2) + (times(high, 3) + times(low, 2))
    return first, second


def moved_exactly(values, table):
    high = values.astype(jnp.bfloat16)
    rest = values - high.astype(jnp.float32)
    middle = rest.astype(jnp.bfloat16)
    low = (rest - middle.astype(jnp.float32)).astype(jnp.bfloat16)
    return (multiply(high, table) + multiply(middle, table)) + multiply(low, table)


def mix(parts, sign):
    (ar, ai), (br, bi), (cr, ci), (dr, di) = parts
    er, ei, gr, gi = ar + cr, ai + ci, ar - cr, ai - ci
    hr, hi, kr, ki = br + dr, bi + di, sign * (br - dr), sign * (bi - di)
    return (er + hr, ei + hi), (gr - ki, gi + kr), (er - hr, ei - hi), (gr + ki, gi - kr)


def aligned(index, size):
    return pl.ds(pl.multiple_of(index * size, size), size)


def phase_of(sent, heard, f, rows, columns):
    hr, hi = heard[0, f : f + 1, columns], heard[1, f : f + 1, columns]
    sr, si = sent[0, rows, f : f + 1], sent[1, rows, f : f + 1]
    return sr * hr - si * hi, sr * hi + si * hr


def halves(first, second):
    low = lax.broadcasted_iota(jnp.int32, first.shape, 1) < lanes // 2
    turn = lambda x: pltpu.roll(x, lanes // 2, 1)
    return jnp.where(low, first, turn(second)), jnp.where(low, turn(first), second)


def whole_kernel(sizes, refs):
    senders, hearers, layers, local, per = sizes
    (spectrum, measured, weights, sent, heard, base, turn_row, turn_column, order, order_back) = refs[:10]
    moved, residual, seen = refs[10:13]
    taken, pieces, box, message, high, low, field, echo, weight = refs[13:22]
    (in_got, in_sent, pair_got, pair_sent, back_got, back_sent, out_got, out_sent) = refs[22:30]
    (weight_got, weight_sent, seen_got, seen_sent, load, kept, left_sent, left_got) = refs[30:]
    groups = hearers * layers
    devices = senders * groups
    slab, wide = spectrum.shape[2:]
    tall = measured.shape[2]
    strip = wide // senders
    rows = slab // chunks
    spans = strip // lanes
    width = base.shape[1]
    planes = 2 * per
    block = layers * rows
    tx, rx, fq = lax.axis_index("tx"), lax.axis_index("rx"), lax.axis_index("freq")
    mine = rx * layers + fq
    me = tx * groups + mine

    def chunk(n):
        return pl.ds(n * rows, rows)

    def remote(source, target, send, receive, device):
        pltpu.make_async_remote_copy(
            src_ref=source, dst_ref=target, send_sem=send, recv_sem=receive, device_id=device, device_id_type=mesh_ids
        ).start()

    def near(source, target, sem):
        pltpu.make_async_copy(source, target, sem).start()

    def settle(ref, sem):
        pltpu.make_async_copy(ref, ref, sem).wait()

    def to_group(make, send, receive):
        def one(d, carry):
            g = lax.rem(mine + d, groups)
            for source, target in make(g):
                remote(source, target, send, receive, (tx, g // layers, g % layers))
            return carry

        lax.fori_loop(1, groups, one, 0)
        for source, target in make(mine):
            near(source, target, receive)

    def to_all(make, send, receive):
        def one(d, carry):
            k = lax.rem(me + d, devices)
            source, target = make(k)
            remote(source, target, send, receive, (k // groups, k // layers % hearers, k % layers))
            return carry

        lax.fori_loop(1, devices, one, 0)
        source, target = make(me)
        near(source, target, receive)

    def pair_of(f, k):
        return pl.ds((f * devices + k) * 2, 2)

    def many(f):
        return pl.ds(f * devices * 2, devices * 2)

    for n in range(chunks):
        to_group(
            lambda g: [(spectrum.at[:, g, chunk(n), :], taken.at[rx, fq, :, chunk(n), :])], in_sent.at[n], in_got.at[n]
        )
    for shift in range(senders):
        other = lax.rem(tx + shift, senders)
        for lc in range(spans):
            source = weights.at[:, aligned(other * spans + lc, lanes)]
            target = weight.at[lc, aligned(tx, tall), :]
            if shift:
                remote(source, target, weight_sent, weight_got, (other, rx, fq))
            else:
                near(source, target, weight_got)
        if shift:
            remote(
                measured.at[:, :, :, aligned(other, strip)],
                seen.at[shift - 1],
                seen_sent,
                seen_got,
                (other, rx, fq),
            )

    def make_pairs(f, n):
        for g in range(layers):

            def body(t, carry):
                row, span = t // (wide // lanes), t % (wide // lanes)
                down, across = aligned(n * (rows // 16) + row, 16), aligned(span, lanes)
                parts = []
                for h in range(hearers):
                    where = aligned(h * (wide // lanes) + span, lanes)
                    zr, zi = phase_of(sent, heard, g * local + f, down, where)
                    ar = taken[h, layers - 1, per - 1, down, across]
                    ai = taken[h, layers - 1, planes - 1, down, across]
                    for j in range(layers * per - 1, -1, -1):
                        ar, ai = ar * zr + ai * zi, ai * zr - ar * zi
                        if j:
                            q, d = divmod(j - 1, per)
                            ar = ar + taken[h, q, d, down, across]
                            ai = ai + taken[h, q, per + d, down, across]
                    parts.append((ar, ai))
                for s, (real, imag) in enumerate(mix(parts, 1.0)):
                    cr, ci = turn_row[2 * s : 2 * s + 1, across], turn_row[2 * s + 1 : 2 * s + 2, across]
                    for c, value in enumerate((real * cr - imag * ci, real * ci + imag * cr)):
                        place = aligned((c * block + g * rows) // 16 + row, 16)
                        high[s, place, across], low[s, place, across] = split(value)
                return carry

            lax.fori_loop(0, rows // 16 * (wide // lanes), body, 0)

        def turn(s, carry):
            first, second = turned(base, high[s, : 2 * block, :], low[s, : 2 * block, :], False)
            field[s, :block, :] = first[:block] - second[block:]
            field[s, block : 2 * block, :] = first[block:] + second[:block]
            return carry

        lax.fori_loop(0, radix, turn, 0)
        for c in range(2):
            for g in range(layers):
                down = pl.ds(c * block + g * rows, rows)
                for p in range(hearers):
                    across = pl.ds(p * lanes, lanes)
                    for lc in range(spans):
                        values = halves(field[2 * lc, down, across], field[2 * lc + 1, down, across])
                        for k in range(senders):
                            place = (f * devices + (k * hearers + p) * layers + g) * 2 + c
                            message[place, chunk(n), lc * lanes : (lc + 1) * lanes] = values[k]

    def send_pairs(f, n):
        to_all(
            lambda k: (message.at[pair_of(f, k), chunk(n), :], box.at[pair_of(f, me), chunk(n), :]),
            pair_sent.at[f, n],
            pair_got.at[f, n],
        )

    def load_echo(f):
        for c in range(2):
            for lc in range(spans):
                for shift in range(senders):
                    source = (
                        seen.at[shift - 1, c, f, :, pl.ds(lc * lanes, lanes)]
                        if shift
                        else measured.at[c, f, :, aligned(tx * spans + lc, lanes)]
                    )
                    other = lax.rem(tx + senders - shift, senders)
                    near(source, echo.at[c, lc, aligned(other, tall), :], load)
        settle(echo, load)

    def send_left(f):
        for c in range(2):
            for lc in range(spans):
                for shift in range(senders):
                    other = lax.rem(tx + senders - shift, senders)
                    source = echo.at[c, lc, aligned(other, tall), :]
                    target = residual.at[c, f, :, aligned(tx * spans + lc, lanes)]
                    if shift:
                        remote(source, target, left_sent, left_got.at[f], (other, rx, fq))
                    else:
                        near(source, target, kept)

    def settle_left():
        settle(echo.at[:, :, pl.ds(0, tall), :], kept)
        if senders > 1:
            settle(echo.at[:, :, pl.ds(tall, tall * (senders - 1)), :], left_sent)

    quarter = devices // radix

    def columns(f):
        def gather(t, carry):
            d, row = t // (slab // 16), t % (slab // 16)
            here, down = aligned(row, 16), aligned(t, 16)
            for lc in range(spans):
                across = slice(lc * lanes, (lc + 1) * lanes)
                parts = [
                    tuple(box[(f * devices + q * quarter + d) * 2 + c, here, across] for c in range(2))
                    for q in range(radix)
                ]
                for s, (real, imag) in enumerate(mix(parts, 1.0)):
                    cr, ci = turn_column[2 * s, down, :], turn_column[2 * s + 1, down, :]
                    for c, value in enumerate((real * cr - imag * ci, real * ci + imag * cr)):
                        place = slice(c * strip + lc * lanes, c * strip + (lc + 1) * lanes)
                        high[s, down, place], low[s, down, place] = split(value)
            return carry

        lax.fori_loop(0, width // 16, gather, 0)

        def middle(s, carry):
            first, second = turned(base, high[s], low[s], True)
            picked = pl.ds(s, width, stride=radix)
            for c in range(2):
                if c:
                    value = first[:, strip:] + second[:, :strip]
                else:
                    value = first[:, :strip] - second[:, strip:]
                value = moved_exactly(value, order_back[...])
                left = []
                for lc in range(spans):
                    across = slice(lc * lanes, (lc + 1) * lanes)
                    part = weight[lc, picked, :] * (echo[c, lc, picked, :] - value[:, across])
                    echo[c, lc, picked, :] = part
                    left.append(part)
                parts = split(jnp.concatenate(left, axis=1))
                for ref, part in zip((high, low), parts):
                    ref[s, :, c * strip : (c + 1) * strip] = multiply(part, order[...]).astype(jnp.bfloat16)
            first, second = turned(base, high[s], low[s], True)
            field[s, :, :strip] = first[:, :strip] + second[:, strip:]
            field[s, :, strip:] = first[:, strip:] - second[:, :strip]
            return carry

        lax.fori_loop(0, radix, middle, 0)

        def scatter(t, carry):
            d, row = t // (slab // 16), t % (slab // 16)
            here, down = aligned(row, 16), aligned(t, 16)
            for lc in range(spans):
                across = slice(lc * lanes, (lc + 1) * lanes)
                parts = []
                for s in range(radix):
                    real = field[s, down, lc * lanes : (lc + 1) * lanes]
                    imag = field[s, down, strip + lc * lanes : strip + (lc + 1) * lanes]
                    cr, ci = turn_column[2 * s, down, :], turn_column[2 * s + 1, down, :]
                    parts.append((real * cr + imag * ci, imag * cr - real * ci))
                for q, values in enumerate(mix(parts, -1.0)):
                    for c in range(2):
                        message[(f * devices + q * quarter + d) * 2 + c, here, across] = values[c]
            return carry

        lax.fori_loop(0, width // 16, scatter, 0)

    def send_back(f, n):
        to_all(
            lambda k: (message.at[pair_of(f, k), chunk(n), :], pieces.at[pair_of(f, me), chunk(n), :]),
            back_sent.at[f, n],
            back_got.at[f, n],
        )

    def gradient(f, n):
        for c in range(2):
            for g in range(layers):
                down = pl.ds(c * block + g * rows, rows)
                for p in range(hearers):
                    for lc in range(spans):
                        across = slice(lc * lanes, (lc + 1) * lanes)
                        where = [(f * devices + (k * hearers + p) * layers + g) * 2 + c for k in range(senders)]
                        values = halves(*[pieces[k, chunk(n), across] for k in where])
                        for k in range(2):
                            spot = (2 * lc + k, down, pl.ds(p * lanes, lanes))
                            high[spot], low[spot] = split(values[k])

        def turn(s, carry):
            first, second = turned(base, high[s, : 2 * block, :], low[s, : 2 * block, :], False)
            field[s, :block, :] = first[:block] + second[block:]
            field[s, block : 2 * block, :] = first[block:] - second[:block]
            return carry

        lax.fori_loop(0, radix, turn, 0)

        def body(t, carry):
            row, span = t // (wide // lanes), t % (wide // lanes)
            across = aligned(span, lanes)
            for g in range(layers):
                spots = [aligned((c * block + g * rows) // 8 + row, 8) for c in range(2)]
                parts = []
                for s in range(radix):
                    real, imag = field[s, spots[0], across], field[s, spots[1], across]
                    cr, ci = turn_row[2 * s : 2 * s + 1, across], turn_row[2 * s + 1 : 2 * s + 2, across]
                    parts.append((real * cr + imag * ci, imag * cr - real * ci))
                for h, values in enumerate(mix(parts, -1.0)):
                    for c in range(2):
                        field[h, spots[c], across] = step_size * values[c]
            here = aligned(n * (rows // 8) + row, 8)
            inner = aligned(span % spans, lanes)
            for h in range(hearers):
                sums = [None] * (layers * per)
                for g in range(layers):
                    where = aligned(h * (wide // lanes) + span, lanes)
                    zr, zi = phase_of(sent, heard, g * local + f, here, where)
                    tr, ti = [field[h, aligned((c * block + g * rows) // 8 + row, 8), across] for c in range(2)]
                    for j in range(layers * per):
                        tr, ti = tr * zr - ti * zi, tr * zi + ti * zr
                        sums[j] = (sums[j][0] + tr, sums[j][1] + ti) if g else (tr, ti)
                for j in range(layers * per):
                    q, d = divmod(j, per)
                    for c in range(2):
                        place = ((h * layers + q) * senders + span // spans) * planes + c * per + d
                        value = sums[j][c]
                        if f:
                            value = value + box[place, here, inner]
                        box[place, here, inner] = value
            return carry

        lax.fori_loop(0, rows // 8 * (wide // lanes), body, 0)

    def send_out(n):
        to_group(
            lambda g: [
                (
                    box.at[pl.ds((g * senders + k) * planes, planes), chunk(n), :],
                    moved.at[:, mine, chunk(n), pl.ds(k * strip, strip)],
                )
                for k in range(senders)
            ],
            out_sent.at[n],
            out_got.at[n],
        )

    for n in range(chunks):
        settle(taken.at[:, :, :, chunk(n), :], in_got.at[n])
        make_pairs(0, n)
        send_pairs(0, n)
        if n:
            for k in range(n):
                for f in range(1, local):
                    send_pairs(f, k)
        for f in range(1, local):
            make_pairs(f, n)
    for f in range(1, local):
        send_pairs(f, chunks - 1)
    settle(weight, weight_got)
    settle(seen, seen_got)
    for f in range(local):
        if f:
            settle_left()
        load_echo(f)
        for n in range(chunks):
            settle(box.at[many(f), chunk(n), :], pair_got.at[f, n])
            settle(message.at[pl.ds(0, (devices - 1) * 2), chunk(n), :], pair_sent.at[f, n])
        columns(f)
        for n in range(chunks):
            send_back(f, n)
        send_left(f)
    for f in range(local):
        for n in range(chunks):
            settle(pieces.at[many(f), chunk(n), :], back_got.at[f, n])
            gradient(f, n)
            if f == local - 1:
                send_out(n)
    settle_left()
    for n in range(chunks):
        settle(spectrum.at[:, pl.ds(0, groups - 1), chunk(n), :], in_sent.at[n])
        for f in range(local):
            settle(message.at[pl.ds(0, (devices - 1) * 2), chunk(n), :], back_sent.at[f, n])
        settle(box.at[pl.ds(0, (groups - 1) * senders * planes), chunk(n), :], out_sent.at[n])
        settle(moved.at[:, :, chunk(n), :], out_got.at[n])
    settle(weights.at[:, pl.ds(0, strip * (senders - 1))], weight_sent)
    settle(seen, seen_sent)
    for f in range(local):
        settle(residual.at[:, f, :, pl.ds(0, strip * (senders - 1))], left_got.at[f])


def per_device_whole(spectrum, measured, wavenumber, send_weight, hear_weight, aperture):
    _, per, rows_sent, rows_heard = spectrum.shape
    local = measured.shape[1]
    senders = lax.axis_size("tx")
    hearers = lax.axis_size("rx")
    layers = lax.axis_size("freq")
    total = rows_sent * senders
    groups = hearers * layers
    slab = rows_sent // groups
    strip = rows_heard // senders
    width = total // radix

    first_row = lax.axis_index("tx") * rows_sent + (lax.axis_index("rx") * layers + lax.axis_index("freq")) * slab
    sent_phase = depth_step * roots(wavenumber, first_row, slab, total).T
    heard_phase = depth_step * roots(wavenumber, 0, total, total)
    sent = jnp.stack([jnp.cos(sent_phase), jnp.sin(sent_phase)])
    heard = jnp.stack([jnp.cos(heard_phase), jnp.sin(heard_phase)])
    cosine, sine = unit_pair(width, width, width)
    base = jnp.stack(split_table(cosine) + split_table(sine))
    turn = jnp.stack(unit_pair(radix, width, total), axis=1).reshape(2 * radix, width) / math.sqrt(total)
    turn_column = jnp.broadcast_to(turn[:, :, None], (2 * radix, width, lanes))

    place = jnp.arange(strip, dtype=jnp.int32)
    source = place % (strip // radix) * radix + place // (strip // radix)
    order = (place[:, None] == source[None, :]).astype(jnp.bfloat16)
    tiles_sent, tiles_heard = aperture.shape
    gate = jnp.repeat(aperture.astype(jnp.float32), rows_heard // tiles_heard, axis=1) * hear_weight[None, :]
    weights = gate[:, None, :] * send_weight.reshape(tiles_sent, -1)[:, :, None]
    weights = weights.reshape(rows_sent, rows_heard)

    sizes = (senders, hearers, layers, local, per)
    anywhere = pl.BlockSpec(memory_space=pl.ANY)
    inside = pl.BlockSpec(memory_space=pltpu.VMEM)
    count = local * senders * groups * 2
    blocks = spectrum.reshape(2 * per, groups, slab, rows_heard)
    floats = lambda *shape: pltpu.VMEM(shape, jnp.float32)
    sems = pltpu.SemaphoreType.DMA
    moved, residual, _ = pl.pallas_call(
        lambda *refs: whole_kernel(sizes, refs),
        in_specs=[anywhere] * 3 + [inside] * 7,
        out_specs=[anywhere] * 3,
        out_shape=[
            jax.ShapeDtypeStruct(blocks.shape, jnp.float32),
            jax.ShapeDtypeStruct(measured.shape, jnp.float32),
            jax.ShapeDtypeStruct((senders - 1, 2, local, rows_sent, strip), jnp.float32),
        ],
        scratch_shapes=[
            floats(hearers, layers, 2 * per, slab, rows_heard),
            floats(count, slab, strip),
            floats(count, slab, strip),
            floats(count, slab, strip),
            pltpu.VMEM((radix, width, width), jnp.bfloat16),
            pltpu.VMEM((radix, width, width), jnp.bfloat16),
            floats(radix, width, width),
            floats(2, strip // lanes, total, lanes),
            floats(strip // lanes, total, lanes),
        ]
        + [sems((chunks,))] * 2
        + [sems((local, chunks))] * 4
        + [sems((chunks,))] * 2
        + [sems] * 7
        + [sems((local,))],
        compiler_params=pltpu.CompilerParams(vmem_limit_bytes=limit, has_side_effects=True),
    )(blocks, measured, weights, sent, heard, base, turn, turn_column, order, order.T)
    return ((blocks + moved).reshape(spectrum.shape), residual)


def fits(mesh, sent, heard):
    senders, hearers, layers = [mesh.shape[axis] for axis in ("tx", "rx", "freq")]
    rows = sent // senders // (hearers * layers)
    return (
        hearers == radix
        and senders == 2
        and sent == heard
        and rows % (16 * chunks) == 0
        and heard // hearers // radix == lanes
    )


def solution(mesh):
    placed = (
        P(None, "freq", "tx", "rx"),
        P(None, "freq", "tx", "rx"),
        P(),
        P("tx"),
        P("rx"),
        P("tx", "rx"),
    )

    def body(*args):
        sent, heard = args[3].shape[0] * mesh.shape["tx"], args[4].shape[0] * mesh.shape["rx"]
        return (per_device_whole if fits(mesh, sent, heard) else per_device)(*args)

    return jax.shard_map(
        body,
        mesh=mesh,
        in_specs=placed,
        out_specs=(P(None, "freq", "tx", "rx"), P(None, "freq", "tx", "rx")),
        check_vma=False,
    )
```

```python
import math

import jax
import jax.numpy as jnp
from jax import lax
from jax.experimental import pallas as pl
from jax.experimental.pallas import tpu as pltpu
from jax.sharding import PartitionSpec as P

depth_step = 2.0
step_size = 0.125
root_floor = 0.25
radix = 4
limit = 67043328


def roots(wavenumber, offset, length, total):
    indices = offset + jnp.arange(length, dtype=jnp.int32)
    signed = jnp.where(indices < total // 2, indices, indices - total)
    waves = 2.0 * jnp.pi / total * signed.astype(jnp.float32)
    squared = (wavenumber * wavenumber)[:, None] - (waves * waves)[None, :]
    return jnp.sqrt(jnp.maximum(squared, 0.0) + root_floor)


def unit_pair(outer, inner, period):
    product = (
        jnp.arange(outer, dtype=jnp.int32)[:, None] * jnp.arange(inner, dtype=jnp.int32)[None, :] % period
    )
    phases = 2.0 * math.pi / period * product.astype(jnp.float32)
    return jnp.cos(phases), jnp.sin(phases)


def dft_tables(total):
    width = total // radix
    base_cos, base_sin = unit_pair(width, width, width)
    turn_cos, turn_sin = unit_pair(radix, width, total)
    scale = 1.0 / math.sqrt(total)
    turn_cos = turn_cos[:, None, :] * scale
    turn_sin = turn_sin[:, None, :] * scale
    return (
        turn_cos * base_cos - turn_sin * base_sin,
        turn_cos * base_sin + turn_sin * base_cos,
    )


def dft(pieces, tables, form, sign):
    (ar, ai), (br, bi), (cr, ci), (dr, di) = [(x[0], x[1]) for x in pieces]
    er, ei, gr, gi = ar + cr, ai + ci, ar - cr, ai - ci
    hr, hi, kr, ki = br + dr, bi + di, sign * (br - dr), sign * (bi - di)
    mixed_real = jnp.stack([er + hr, gr - ki, er - hr, gr + ki])
    mixed_imag = jnp.stack([ei + hi, gi + kr, ei - hi, gi - kr])
    mixed = jnp.stack([mixed_real, mixed_imag], axis=1)
    cosine, sine = tables
    first = jnp.einsum(form, cosine, mixed, precision=lax.Precision.HIGH)
    second = jnp.einsum(form, sine, mixed, precision=lax.Precision.HIGH)
    return jnp.stack(
        [
            first[:, :, 0] - sign * second[:, :, 1],
            first[:, :, 1] + sign * second[:, :, 0],
        ]
    )


def unmix(done, blocks):
    total = done.shape[1] * done.shape[2]
    rows = total // math.prod(blocks)
    freqs, width = done.shape[3:]
    done = jnp.transpose(done, (2, 1, 0, 3, 4)).reshape((math.prod(blocks), rows, 2, freqs, width))
    return jnp.transpose(done, (0, 2, 3, 1, 4)).reshape(tuple(blocks) + (2, freqs, rows, width))


def quarters(chunks, axis):
    count = chunks.shape[0]
    if count >= radix and count % radix == 0:
        step = count // radix
        return [
            jnp.concatenate([chunks[q * step + k] for k in range(step)], axis=axis) for q in range(radix)
        ]
    whole = jnp.concatenate([chunks[k] for k in range(count)], axis=axis)
    return jnp.split(whole, radix, axis=axis)


def exchange(values, axes):
    return lax.all_to_all(values, axes, split_axis=0, concat_axis=0, tiled=True)


def pair_kernel(layers, sent, heard, out):
    depth, rows = layers.shape[1:3]
    for f in range(out.shape[1]):
        hr = heard[0, f : f + 1, :]
        hi = heard[1, f : f + 1, :]
        for start in range(0, rows, 8):
            block = slice(start, start + 8)
            sr = sent[0, block, f : f + 1]
            si = sent[1, block, f : f + 1]
            zr = sr * hr - si * hi
            zi = -(sr * hi + si * hr)
            ar = layers[0, depth - 1, block, :]
            ai = layers[1, depth - 1, block, :]
            for j in range(depth - 1, -1, -1):
                ar, ai = ar * zr - ai * zi, ar * zi + ai * zr
                if j:
                    ar = ar + layers[0, j - 1, block, :]
                    ai = ai + layers[1, j - 1, block, :]
            out[0, f, block, :] = ar
            out[1, f, block, :] = ai


def gradient_kernel(pieces, sent, heard, out):
    freqs, rows = pieces.shape[1:3]
    depth = out.shape[1]
    for start in range(0, rows, 8):
        block = slice(start, start + 8)
        sums = [None] * depth
        for f in range(freqs):
            hr = heard[0, f : f + 1, :]
            hi = heard[1, f : f + 1, :]
            sr = sent[0, block, f : f + 1]
            si = sent[1, block, f : f + 1]
            zr = sr * hr - si * hi
            zi = sr * hi + si * hr
            tr = step_size * pieces[0, f, block, :]
            ti = step_size * pieces[1, f, block, :]
            for j in range(depth):
                tr, ti = tr * zr - ti * zi, tr * zi + ti * zr
                if f:
                    sums[j] = (sums[j][0] + tr, sums[j][1] + ti)
                else:
                    sums[j] = (tr, ti)
        for j in range(depth):
            out[0, j, block, :] = sums[j][0]
            out[1, j, block, :] = sums[j][1]


def pointwise(kernel, values, sent, heard, planes):
    _, count, rows, width = values.shape
    freqs = heard.shape[1]
    height = min(rows, 32)
    lanes = min(width, 128)
    return pl.pallas_call(
        kernel,
        grid=(rows // height, width // lanes),
        in_specs=[
            pl.BlockSpec((2, count, height, lanes), lambda i, k: (0, 0, i, k)),
            pl.BlockSpec((2, height, freqs), lambda i, k: (0, i, 0)),
            pl.BlockSpec((2, freqs, lanes), lambda i, k: (0, 0, k)),
        ],
        out_specs=pl.BlockSpec((2, planes, height, lanes), lambda i, k: (0, 0, i, k)),
        out_shape=jax.ShapeDtypeStruct((2, planes, rows, width), jnp.float32),
    )(values, sent, heard)


def per_device(spectrum, measured, wavenumber, send_weight, hear_weight, aperture):
    _, depth_local, rows_sent, rows_heard = spectrum.shape
    freq_local = measured.shape[1]
    freq_total = wavenumber.shape[0]
    senders = lax.axis_size("tx")
    hearers = lax.axis_size("rx")
    layers = lax.axis_size("freq")
    depth = depth_local * layers
    total_sent = rows_sent * senders
    total_heard = rows_heard * hearers
    slab = rows_sent // layers
    strip = rows_heard // senders
    band = rows_sent // hearers

    first_row = lax.axis_index("tx") * rows_sent + lax.axis_index("freq") * slab
    sent_phase = depth_step * roots(wavenumber, first_row, slab, total_sent).T
    heard_phase = depth_step * roots(wavenumber, lax.axis_index("rx") * rows_heard, rows_heard, total_heard)
    sent = jnp.stack([jnp.cos(sent_phase), jnp.sin(sent_phase)])
    heard = jnp.stack([jnp.cos(heard_phase), jnp.sin(heard_phase)])
    tables_sent = dft_tables(total_sent)
    tables_heard = tables_sent if total_heard == total_sent else dft_tables(total_heard)
    near = "qsm,qcfmw->qscfw"
    far = "qsm,qcfwm->qscfw"

    split = spectrum.reshape(2, depth_local, layers, slab, rows_heard)
    split = exchange(jnp.transpose(split, (2, 0, 1, 3, 4)), "freq")
    stacked = jnp.transpose(split, (1, 0, 2, 3, 4)).reshape(2, depth, slab, rows_heard)
    pair = pointwise(pair_kernel, stacked, sent, heard, freq_total)

    pair = pair.reshape(2, layers, freq_local, slab, senders, strip)
    pair = jnp.transpose(pair, (4, 1, 0, 2, 3, 5)).reshape(senders * layers, 2, freq_local, slab, strip)
    pair = exchange(pair, ("tx", "freq"))
    done = dft(quarters(pair, 2), tables_sent, near, 1.0)
    done = exchange(unmix(done, (senders * hearers,)), ("tx", "rx"))
    done = done.reshape((senders, hearers) + done.shape[1:])
    done = jnp.swapaxes(done, 0, 1).reshape((senders * hearers,) + done.shape[2:])
    done = dft(quarters(done, 3), tables_heard, far, 1.0)
    done = exchange(unmix(done, (hearers,)), "rx")
    field = jnp.transpose(done, (1, 2, 0, 4, 3)).reshape(2, freq_local, rows_sent, rows_heard)

    tiles_sent, tiles_heard = aperture.shape
    gate = aperture.astype(jnp.float32)
    weights = (
        send_weight.reshape(tiles_sent, -1)[:, :, None, None]
        * gate[:, None, :, None]
        * hear_weight.reshape(tiles_heard, -1)[None, None, :, :]
    ).reshape(rows_sent, rows_heard)
    residual = weights[None, None] * (measured - field)

    back = residual.reshape(2, freq_local, hearers, band, rows_heard)
    back = exchange(jnp.transpose(back, (2, 0, 1, 3, 4)), "rx")
    done = dft(quarters(back, 3), tables_heard, far, -1.0)
    done = unmix(done, (hearers, senders))
    done = jnp.swapaxes(done, 0, 1).reshape((senders * hearers,) + done.shape[2:])
    done = exchange(done, ("tx", "rx"))
    done = dft(quarters(done, 3), tables_sent, far, -1.0)
    done = exchange(unmix(done, (senders * layers,)), ("tx", "freq"))
    done = done.reshape(senders, layers, 2, freq_local, slab, strip)
    pieces = jnp.transpose(done, (2, 1, 3, 4, 0, 5)).reshape(2, freq_total, slab, rows_heard)

    gradient = pointwise(gradient_kernel, pieces, sent, heard, depth)
    gradient = gradient.reshape(2, layers, depth_local, slab, rows_heard)
    gradient = exchange(jnp.transpose(gradient, (1, 0, 2, 3, 4)), "freq")
    gradient = jnp.transpose(gradient, (1, 2, 0, 3, 4)).reshape(spectrum.shape)
    return (spectrum + gradient, residual)


lanes = 128
chunks = 2
mesh_ids = pl.DeviceIdType.MESH


def split(values):
    high = values.astype(jnp.bfloat16)
    return high, (values - high.astype(jnp.float32)).astype(jnp.bfloat16)


def multiply(left, right):
    return jnp.dot(left, right, preferred_element_type=jnp.float32)


def turned(base, high, low, left):
    def times(values, kind):
        return multiply(base[kind], values) if left else multiply(values, base[kind])

    first = times(high, 0) + (times(high, 1) + times(low, 0))
    second = times(high, 2) + (times(high, 3) + times(low, 2))
    return first, second


def moved_exactly(values, table):
    high = values.astype(jnp.bfloat16)
    rest = values - high.astype(jnp.float32)
    middle = rest.astype(jnp.bfloat16)
    low = (rest - middle.astype(jnp.float32)).astype(jnp.bfloat16)
    return (multiply(high, table) + multiply(middle, table)) + multiply(low, table)


def mix(parts, sign):
    (ar, ai), (br, bi), (cr, ci), (dr, di) = parts
    er, ei, gr, gi = ar + cr, ai + ci, ar - cr, ai - ci
    hr, hi, kr, ki = br + dr, bi + di, sign * (br - dr), sign * (bi - di)
    return (er + hr, ei + hi), (gr - ki, gi + kr), (er - hr, ei - hi), (gr + ki, gi - kr)


def aligned(index, size):
    return pl.ds(pl.multiple_of(index * size, size), size)


def phase_of(sent, heard, f, rows, columns):
    hr, hi = heard[0, f : f + 1, columns], heard[1, f : f + 1, columns]
    sr, si = sent[0, rows, f : f + 1], sent[1, rows, f : f + 1]
    return sr * hr - si * hi, sr * hi + si * hr


def halves(first, second):
    low = lax.broadcasted_iota(jnp.int32, first.shape, 1) < lanes // 2
    turn = lambda x: pltpu.roll(x, lanes // 2, 1)
    return jnp.where(low, first, turn(second)), jnp.where(low, turn(first), second)


def whole_kernel(sizes, refs):
    senders, hearers, layers, local, per = sizes
    spectrum, measured, weights, wavenumber = refs[:4]
    moved, residual, seen = refs[4:7]
    taken, pieces, box, message, high, low, field, echo, weight = refs[7:16]
    sent, heard, base, turn_row, turn_column, order, order_back = refs[16:23]
    (in_got, in_sent, pair_got, pair_sent, back_got, back_sent, out_got, out_sent) = refs[23:31]
    (weight_got, weight_sent, seen_got, seen_sent, load, kept, left_sent, left_got) = refs[31:]
    groups = hearers * layers
    devices = senders * groups
    slab, wide = spectrum.shape[2:]
    tall = measured.shape[2]
    strip = wide // senders
    rows = slab // chunks
    spans = strip // lanes
    width = high.shape[1]
    planes = 2 * per
    block = layers * rows
    tx, rx, fq = lax.axis_index("tx"), lax.axis_index("rx"), lax.axis_index("freq")
    mine = rx * layers + fq
    me = tx * groups + mine

    def chunk(n):
        return pl.ds(n * rows, rows)

    def remote(source, target, send, receive, device):
        pltpu.make_async_remote_copy(
            src_ref=source, dst_ref=target, send_sem=send, recv_sem=receive, device_id=device, device_id_type=mesh_ids
        ).start()

    def near(source, target, sem):
        pltpu.make_async_copy(source, target, sem).start()

    def settle(ref, sem):
        pltpu.make_async_copy(ref, ref, sem).wait()

    def to_group(make, send, receive):
        def far(d, carry):
            j = lax.rem(fq + d, layers)
            for there in ((rx + 2) % hearers, 3 - rx, rx + 1 - 2 * (rx % 2)):
                for source, target in make(there * layers + j):
                    remote(source, target, send, receive, (tx, there, j))
            return carry

        def close(d, carry):
            j = lax.rem(fq + d, layers)
            for source, target in make(rx * layers + j):
                remote(source, target, send, receive, (tx, rx, j))
            return carry

        lax.fori_loop(0, layers, far, 0)
        lax.fori_loop(1, layers, close, 0)
        for source, target in make(mine):
            near(source, target, receive)

    def to_all(make, send, receive):
        def place(j, there):
            return (j // layers * hearers + there) * layers + j % layers

        def far(d, carry):
            j = lax.rem(tx * layers + fq + d, senders * layers)
            for there in ((rx + 2) % hearers, 3 - rx, rx + 1 - 2 * (rx % 2)):
                source, target = make(place(j, there))
                remote(source, target, send, receive, (j // layers, there, j % layers))
            return carry

        def close(d, carry):
            j = lax.rem(tx * layers + fq + d, senders * layers)
            source, target = make(place(j, rx))
            remote(source, target, send, receive, (j // layers, rx, j % layers))
            return carry

        lax.fori_loop(0, senders * layers, far, 0)
        lax.fori_loop(1, senders * layers, close, 0)
        source, target = make(me)
        near(source, target, receive)

    def pair_of(f, k):
        return pl.ds((f * devices + k) * 2, 2)

    def many(f):
        return pl.ds(f * devices * 2, devices * 2)

    for n in range(chunks):
        to_group(
            lambda g: [(spectrum.at[:, g, chunk(n), :], taken.at[rx, fq, :, chunk(n), :])], in_sent.at[n], in_got.at[n]
        )
    for shift in range(senders):
        other = lax.rem(tx + shift, senders)
        for lc in range(spans):
            source = weights.at[:, aligned(other * spans + lc, lanes)]
            target = weight.at[lc, aligned(tx, tall), :]
            if shift:
                remote(source, target, weight_sent, weight_got, (other, rx, fq))
            else:
                near(source, target, weight_got)
        if shift:
            remote(
                measured.at[:, :, :, aligned(other, strip)],
                seen.at[shift - 1],
                seen_sent,
                seen_got,
                (other, rx, fq),
            )

    total = width * radix

    def make_phases(ref, numbers, offset, axis, shape):
        indices = offset + lax.broadcasted_iota(jnp.int32, shape, axis)
        signed = jnp.where(indices < total // 2, indices, indices - total)
        waves = 2.0 * jnp.pi / total * signed.astype(jnp.float32)
        phase = depth_step * jnp.sqrt(jnp.maximum(numbers * numbers - waves * waves, 0.0) + root_floor)
        ref[0], ref[1] = jnp.cos(phase), jnp.sin(phase)

    def make_tables():
        numbers = wavenumber[...]
        freqs = numbers.shape[1]
        square = (freqs, freqs)
        same = lax.broadcasted_iota(jnp.int32, square, 0) == lax.broadcasted_iota(jnp.int32, square, 1)
        tall_numbers = jnp.sum(jnp.where(same, jnp.broadcast_to(numbers, square), 0.0), axis=1, keepdims=True)
        make_phases(sent, numbers, tx * tall + mine * slab, 0, (slab, freqs))
        make_phases(heard, tall_numbers, 0, 1, (freqs, total))
        scale = 1.0 / math.sqrt(total)

        def angles(product, period):
            return 2.0 * math.pi / period * product.astype(jnp.float32)

        def fill(t, carry):
            down = aligned(t, 16)
            row = t * 16 + lax.broadcasted_iota(jnp.int32, (16, width), 0)
            product = jnp.bitwise_and(row * lax.broadcasted_iota(jnp.int32, (16, width), 1), width - 1)
            phase = angles(product, width)
            for k, values in enumerate((jnp.cos(phase), jnp.sin(phase))):
                base[2 * k, down, :], base[2 * k + 1, down, :] = split(values)
            row = row[:, :lanes]
            for s in range(radix):
                phase = angles(s * row, total)
                turn_column[2 * s, down, :] = jnp.cos(phase) * scale
                turn_column[2 * s + 1, down, :] = jnp.sin(phase) * scale
            return carry

        lax.fori_loop(0, width // 16, fill, 0)
        for s in range(radix):
            phase = angles(s * lax.broadcasted_iota(jnp.int32, (1, width), 1), total)
            turn_row[2 * s : 2 * s + 1, :] = jnp.cos(phase) * scale
            turn_row[2 * s + 1 : 2 * s + 2, :] = jnp.sin(phase) * scale
        part = strip // radix
        for ref, axis in ((order, 0), (order_back, 1)):
            natural = lax.broadcasted_iota(jnp.int32, (strip, strip), axis)
            place = lax.broadcasted_iota(jnp.int32, (strip, strip), 1 - axis)
            source = jnp.bitwise_and(place, part - 1) * radix + place // part
            ref[...] = jnp.where(natural == source, 1.0, 0.0).astype(jnp.bfloat16)

    make_tables()

    def make_pairs(f, n):
        for g in range(layers):

            def body(t, carry):
                row, span = t // (wide // lanes), t % (wide // lanes)
                down, across = aligned(n * (rows // 16) + row, 16), aligned(span, lanes)
                parts = []
                for h in range(hearers):
                    where = aligned(h * (wide // lanes) + span, lanes)
                    zr, zi = phase_of(sent, heard, g * local + f, down, where)
                    ar = taken[h, layers - 1, per - 1, down, across]
                    ai = taken[h, layers - 1, planes - 1, down, across]
                    for j in range(layers * per - 1, -1, -1):
                        ar, ai = ar * zr + ai * zi, ai * zr - ar * zi
                        if j:
                            q, d = divmod(j - 1, per)
                            ar = ar + taken[h, q, d, down, across]
                            ai = ai + taken[h, q, per + d, down, across]
                    parts.append((ar, ai))
                for s, (real, imag) in enumerate(mix(parts, 1.0)):
                    cr, ci = turn_row[2 * s : 2 * s + 1, across], turn_row[2 * s + 1 : 2 * s + 2, across]
                    for c, value in enumerate((real * cr - imag * ci, real * ci + imag * cr)):
                        place = aligned((c * block + g * rows) // 16 + row, 16)
                        high[s, place, across], low[s, place, across] = split(value)
                return carry

            lax.fori_loop(0, rows // 16 * (wide // lanes), body, 0)

        def turn(s, carry):
            first, second = turned(base, high[s, : 2 * block, :], low[s, : 2 * block, :], False)
            field[s, :block, :] = first[:block] - second[block:]
            field[s, block : 2 * block, :] = first[block:] + second[:block]
            return carry

        lax.fori_loop(0, radix, turn, 0)
        for c in range(2):
            for g in range(layers):
                down = pl.ds(c * block + g * rows, rows)
                for p in range(hearers):
                    across = pl.ds(p * lanes, lanes)
                    for lc in range(spans):
                        values = halves(field[2 * lc, down, across], field[2 * lc + 1, down, across])
                        for k in range(senders):
                            place = (f * devices + (k * hearers + p) * layers + g) * 2 + c
                            message[place, chunk(n), lc * lanes : (lc + 1) * lanes] = values[k]

    def send_pairs(f, n):
        to_all(
            lambda k: (message.at[pair_of(f, k), chunk(n), :], box.at[pair_of(f, me), chunk(n), :]),
            pair_sent.at[f, n],
            pair_got.at[f, n],
        )

    def load_echo(f):
        for c in range(2):
            for lc in range(spans):
                for shift in range(senders):
                    source = (
                        seen.at[shift - 1, c, f, :, pl.ds(lc * lanes, lanes)]
                        if shift
                        else measured.at[c, f, :, aligned(tx * spans + lc, lanes)]
                    )
                    other = lax.rem(tx + senders - shift, senders)
                    near(source, echo.at[f, c, lc, aligned(other, tall), :], load.at[f])

    def send_left(f):
        for c in range(2):
            for lc in range(spans):
                for shift in range(senders):
                    other = lax.rem(tx + senders - shift, senders)
                    source = echo.at[f, c, lc, aligned(other, tall), :]
                    target = residual.at[c, f, :, aligned(tx * spans + lc, lanes)]
                    if shift:
                        remote(source, target, left_sent.at[f], left_got.at[f], (other, rx, fq))
                    else:
                        near(source, target, kept.at[f])

    def settle_left(f):
        settle(echo.at[f, :, :, pl.ds(0, tall), :], kept.at[f])
        settle(echo.at[f, :, :, pl.ds(tall, tall * (senders - 1)), :], left_sent.at[f])

    quarter = devices // radix

    def columns(f):
        def gather(t, carry):
            d, row = t // (slab // 16), t % (slab // 16)
            here, down = aligned(row, 16), aligned(t, 16)
            for lc in range(spans):
                across = slice(lc * lanes, (lc + 1) * lanes)
                parts = [
                    tuple(box[(f * devices + q * quarter + d) * 2 + c, here, across] for c in range(2))
                    for q in range(radix)
                ]
                for s, (real, imag) in enumerate(mix(parts, 1.0)):
                    cr, ci = turn_column[2 * s, down, :], turn_column[2 * s + 1, down, :]
                    for c, value in enumerate((real * cr - imag * ci, real * ci + imag * cr)):
                        place = slice(c * strip + lc * lanes, c * strip + (lc + 1) * lanes)
                        high[s, down, place], low[s, down, place] = split(value)
            return carry

        lax.fori_loop(0, width // 16, gather, 0)

        def middle(s, carry):
            first, second = turned(base, high[s], low[s], True)
            picked = pl.ds(s, width, stride=radix)
            for c in range(2):
                if c:
                    value = first[:, strip:] + second[:, :strip]
                else:
                    value = first[:, :strip] - second[:, strip:]
                value = moved_exactly(value, order_back[...])
                left = []
                for lc in range(spans):
                    across = slice(lc * lanes, (lc + 1) * lanes)
                    part = weight[lc, picked, :] * (echo[f, c, lc, picked, :] - value[:, across])
                    echo[f, c, lc, picked, :] = part
                    left.append(part)
                parts = split(jnp.concatenate(left, axis=1))
                for ref, part in zip((high, low), parts):
                    ref[s, :, c * strip : (c + 1) * strip] = multiply(part, order[...]).astype(jnp.bfloat16)
            first, second = turned(base, high[s], low[s], True)
            field[s, :, :strip] = first[:, :strip] + second[:, strip:]
            field[s, :, strip:] = first[:, strip:] - second[:, :strip]
            return carry

        lax.fori_loop(0, radix, middle, 0)

        def scatter(t, carry):
            d, row = t // (slab // 16), t % (slab // 16)
            here, down = aligned(row, 16), aligned(t, 16)
            for lc in range(spans):
                across = slice(lc * lanes, (lc + 1) * lanes)
                parts = []
                for s in range(radix):
                    real = field[s, down, lc * lanes : (lc + 1) * lanes]
                    imag = field[s, down, strip + lc * lanes : strip + (lc + 1) * lanes]
                    cr, ci = turn_column[2 * s, down, :], turn_column[2 * s + 1, down, :]
                    parts.append((real * cr + imag * ci, imag * cr - real * ci))
                for q, values in enumerate(mix(parts, -1.0)):
                    for c in range(2):
                        message[(f * devices + q * quarter + d) * 2 + c, here, across] = values[c]
            return carry

        lax.fori_loop(0, width // 16, scatter, 0)

    def send_back(f, n):
        to_all(
            lambda k: (message.at[pair_of(f, k), chunk(n), :], pieces.at[pair_of(f, me), chunk(n), :]),
            back_sent.at[f, n],
            back_got.at[f, n],
        )

    def gradient(f, n):
        for c in range(2):
            for g in range(layers):
                down = pl.ds(c * block + g * rows, rows)
                for p in range(hearers):
                    for lc in range(spans):
                        across = slice(lc * lanes, (lc + 1) * lanes)
                        where = [(f * devices + (k * hearers + p) * layers + g) * 2 + c for k in range(senders)]
                        values = halves(*[pieces[k, chunk(n), across] for k in where])
                        for k in range(2):
                            spot = (2 * lc + k, down, pl.ds(p * lanes, lanes))
                            high[spot], low[spot] = split(values[k])

        def turn(s, carry):
            first, second = turned(base, high[s, : 2 * block, :], low[s, : 2 * block, :], False)
            field[s, :block, :] = first[:block] + second[block:]
            field[s, block : 2 * block, :] = first[block:] - second[:block]
            return carry

        lax.fori_loop(0, radix, turn, 0)

        def body(t, carry):
            row, span = t // (wide // lanes), t % (wide // lanes)
            across = aligned(span, lanes)
            for g in range(layers):
                spots = [aligned((c * block + g * rows) // 8 + row, 8) for c in range(2)]
                parts = []
                for s in range(radix):
                    real, imag = field[s, spots[0], across], field[s, spots[1], across]
                    cr, ci = turn_row[2 * s : 2 * s + 1, across], turn_row[2 * s + 1 : 2 * s + 2, across]
                    parts.append((real * cr + imag * ci, imag * cr - real * ci))
                for h, values in enumerate(mix(parts, -1.0)):
                    for c in range(2):
                        field[h, spots[c], across] = step_size * values[c]
            here = aligned(n * (rows // 8) + row, 8)
            inner = aligned(span % spans, lanes)
            for h in range(hearers):
                sums = [None] * (layers * per)
                for g in range(layers):
                    where = aligned(h * (wide // lanes) + span, lanes)
                    zr, zi = phase_of(sent, heard, g * local + f, here, where)
                    tr, ti = [field[h, aligned((c * block + g * rows) // 8 + row, 8), across] for c in range(2)]
                    for j in range(layers * per):
                        tr, ti = tr * zr - ti * zi, tr * zi + ti * zr
                        sums[j] = (sums[j][0] + tr, sums[j][1] + ti) if g else (tr, ti)
                for j in range(layers * per):
                    q, d = divmod(j, per)
                    for c in range(2):
                        place = ((h * layers + q) * senders + span // spans) * planes + c * per + d
                        value = sums[j][c]
                        if f:
                            value = value + box[place, here, inner]
                        box[place, here, inner] = value
            return carry

        lax.fori_loop(0, rows // 8 * (wide // lanes), body, 0)

    def send_out(n):
        to_group(
            lambda g: [
                (
                    box.at[pl.ds((g * senders + k) * planes, planes), chunk(n), :],
                    moved.at[:, mine, chunk(n), pl.ds(k * strip, strip)],
                )
                for k in range(senders)
            ],
            out_sent.at[n],
            out_got.at[n],
        )

    for n in range(chunks):
        settle(taken.at[:, :, :, chunk(n), :], in_got.at[n])
        make_pairs(0, n)
        send_pairs(0, n)
        if n:
            for k in range(n):
                for f in range(1, local):
                    send_pairs(f, k)
        for f in range(1, local):
            make_pairs(f, n)
    for f in range(1, local):
        send_pairs(f, chunks - 1)
    settle(weight, weight_got)
    settle(seen, seen_got)
    for f in range(local):
        load_echo(f)
    for f in range(local):
        settle(echo.at[f], load.at[f])
        for n in range(chunks):
            settle(box.at[many(f), chunk(n), :], pair_got.at[f, n])
            settle(message.at[pl.ds(0, (devices - 1) * 2), chunk(n), :], pair_sent.at[f, n])
        columns(f)
        for n in range(chunks):
            send_back(f, n)
    for f in range(local):
        send_left(f)
    for f in range(local):
        for n in range(chunks):
            settle(pieces.at[many(f), chunk(n), :], back_got.at[f, n])
            gradient(f, n)
            if f == local - 1:
                send_out(n)
    for f in range(local):
        settle_left(f)
    for n in range(chunks):
        settle(spectrum.at[:, pl.ds(0, groups - 1), chunk(n), :], in_sent.at[n])
        for f in range(local):
            settle(message.at[pl.ds(0, (devices - 1) * 2), chunk(n), :], back_sent.at[f, n])
        settle(box.at[pl.ds(0, (groups - 1) * senders * planes), chunk(n), :], out_sent.at[n])
        settle(moved.at[:, :, chunk(n), :], out_got.at[n])
    settle(weights.at[:, pl.ds(0, strip * (senders - 1))], weight_sent)
    settle(seen, seen_sent)
    for f in range(local):
        settle(residual.at[:, f, :, pl.ds(0, strip * (senders - 1))], left_got.at[f])


def per_device_whole(spectrum, measured, wavenumber, send_weight, hear_weight, aperture):
    _, per, rows_sent, rows_heard = spectrum.shape
    local = measured.shape[1]
    senders = lax.axis_size("tx")
    hearers = lax.axis_size("rx")
    layers = lax.axis_size("freq")
    total = rows_sent * senders
    groups = hearers * layers
    slab = rows_sent // groups
    strip = rows_heard // senders
    width = total // radix

    tiles_sent, tiles_heard = aperture.shape
    gate = jnp.repeat(aperture.astype(jnp.float32), rows_heard // tiles_heard, axis=1) * hear_weight[None, :]
    weights = gate[:, None, :] * send_weight.reshape(tiles_sent, -1)[:, :, None]
    weights = weights.reshape(rows_sent, rows_heard)

    sizes = (senders, hearers, layers, local, per)
    anywhere = pl.BlockSpec(memory_space=pl.ANY)
    inside = pl.BlockSpec(memory_space=pltpu.VMEM)
    count = local * senders * groups * 2
    freqs = local * layers
    blocks = spectrum.reshape(2 * per, groups, slab, rows_heard)
    floats = lambda *shape: pltpu.VMEM(shape, jnp.float32)
    sems = pltpu.SemaphoreType.DMA
    moved, residual, _ = pl.pallas_call(
        lambda *refs: whole_kernel(sizes, refs),
        in_specs=[anywhere] * 3 + [inside],
        out_specs=[anywhere] * 3,
        out_shape=[
            jax.ShapeDtypeStruct(blocks.shape, jnp.float32),
            jax.ShapeDtypeStruct(measured.shape, jnp.float32),
            jax.ShapeDtypeStruct((senders - 1, 2, local, rows_sent, strip), jnp.float32),
        ],
        scratch_shapes=[
            floats(hearers, layers, 2 * per, slab, rows_heard),
            floats(count, slab, strip),
            floats(count, slab, strip),
            floats(count, slab, strip),
            pltpu.VMEM((radix, width, width), jnp.bfloat16),
            pltpu.VMEM((radix, width, width), jnp.bfloat16),
            floats(radix, width, width),
            floats(local, 2, strip // lanes, total, lanes),
            floats(strip // lanes, total, lanes),
            floats(2, slab, freqs),
            floats(2, freqs, total),
            pltpu.VMEM((4, width, width), jnp.bfloat16),
            floats(2 * radix, width),
            floats(2 * radix, width, lanes),
            pltpu.VMEM((strip, strip), jnp.bfloat16),
            pltpu.VMEM((strip, strip), jnp.bfloat16),
        ]
        + [sems((chunks,))] * 2
        + [sems((local, chunks))] * 4
        + [sems((chunks,))] * 2
        + [sems] * 4
        + [sems((local,))] * 4,
        compiler_params=pltpu.CompilerParams(vmem_limit_bytes=limit, has_side_effects=True),
    )(blocks, measured, weights, wavenumber.reshape(1, -1))
    return ((blocks + moved).reshape(spectrum.shape), residual)


def fits(mesh, sent, heard):
    senders, hearers, layers = [mesh.shape[axis] for axis in ("tx", "rx", "freq")]
    rows = sent // senders // (hearers * layers)
    return (
        hearers == radix
        and senders == 2
        and sent == heard
        and rows % (16 * chunks) == 0
        and heard // hearers // radix == lanes
        and heard & (heard - 1) == 0
    )


def solution(mesh):
    placed = (
        P(None, "freq", "tx", "rx"),
        P(None, "freq", "tx", "rx"),
        P(),
        P("tx"),
        P("rx"),
        P("tx", "rx"),
    )

    def body(*args):
        sent, heard = args[3].shape[0] * mesh.shape["tx"], args[4].shape[0] * mesh.shape["rx"]
        return (per_device_whole if fits(mesh, sent, heard) else per_device)(*args)

    return jax.shard_map(
        body,
        mesh=mesh,
        in_specs=placed,
        out_specs=(P(None, "freq", "tx", "rx"), P(None, "freq", "tx", "rx")),
        check_vma=False,
    )
```

```python
import math

import jax
import jax.numpy as jnp
from jax import lax
from jax.experimental import pallas as pl
from jax.experimental.pallas import tpu as pltpu
from jax.sharding import PartitionSpec as P

depth_step = 2.0
step_size = 0.125
root_floor = 0.25
radix = 4
limit = 54 << 20


def roots(wavenumber, offset, length, total):
    indices = offset + jnp.arange(length, dtype=jnp.int32)
    signed = jnp.where(indices < total // 2, indices, indices - total)
    waves = 2.0 * jnp.pi / total * signed.astype(jnp.float32)
    squared = (wavenumber * wavenumber)[:, None] - (waves * waves)[None, :]
    return jnp.sqrt(jnp.maximum(squared, 0.0) + root_floor)


def unit_pair(outer, inner, period):
    product = (
        jnp.arange(outer, dtype=jnp.int32)[:, None] * jnp.arange(inner, dtype=jnp.int32)[None, :] % period
    )
    phases = 2.0 * math.pi / period * product.astype(jnp.float32)
    return jnp.cos(phases), jnp.sin(phases)


def dft_tables(total):
    width = total // radix
    base_cos, base_sin = unit_pair(width, width, width)
    turn_cos, turn_sin = unit_pair(radix, width, total)
    scale = 1.0 / math.sqrt(total)
    turn_cos = turn_cos[:, None, :] * scale
    turn_sin = turn_sin[:, None, :] * scale
    return (
        turn_cos * base_cos - turn_sin * base_sin,
        turn_cos * base_sin + turn_sin * base_cos,
    )


def dft(pieces, tables, form, sign):
    (ar, ai), (br, bi), (cr, ci), (dr, di) = [(x[0], x[1]) for x in pieces]
    er, ei, gr, gi = ar + cr, ai + ci, ar - cr, ai - ci
    hr, hi, kr, ki = br + dr, bi + di, sign * (br - dr), sign * (bi - di)
    mixed_real = jnp.stack([er + hr, gr - ki, er - hr, gr + ki])
    mixed_imag = jnp.stack([ei + hi, gi + kr, ei - hi, gi - kr])
    mixed = jnp.stack([mixed_real, mixed_imag], axis=1)
    cosine, sine = tables
    first = jnp.einsum(form, cosine, mixed, precision=lax.Precision.HIGH)
    second = jnp.einsum(form, sine, mixed, precision=lax.Precision.HIGH)
    return jnp.stack(
        [
            first[:, :, 0] - sign * second[:, :, 1],
            first[:, :, 1] + sign * second[:, :, 0],
        ]
    )


def unmix(done, blocks):
    total = done.shape[1] * done.shape[2]
    rows = total // math.prod(blocks)
    freqs, width = done.shape[3:]
    done = jnp.transpose(done, (2, 1, 0, 3, 4)).reshape((math.prod(blocks), rows, 2, freqs, width))
    return jnp.transpose(done, (0, 2, 3, 1, 4)).reshape(tuple(blocks) + (2, freqs, rows, width))


def quarters(chunks, axis):
    count = chunks.shape[0]
    if count >= radix and count % radix == 0:
        step = count // radix
        return [
            jnp.concatenate([chunks[q * step + k] for k in range(step)], axis=axis) for q in range(radix)
        ]
    whole = jnp.concatenate([chunks[k] for k in range(count)], axis=axis)
    return jnp.split(whole, radix, axis=axis)


def exchange(values, axes):
    return lax.all_to_all(values, axes, split_axis=0, concat_axis=0, tiled=True)


def pair_kernel(layers, sent, heard, out):
    depth, rows = layers.shape[1:3]
    for f in range(out.shape[1]):
        hr = heard[0, f : f + 1, :]
        hi = heard[1, f : f + 1, :]
        for start in range(0, rows, 8):
            block = slice(start, start + 8)
            sr = sent[0, block, f : f + 1]
            si = sent[1, block, f : f + 1]
            zr = sr * hr - si * hi
            zi = -(sr * hi + si * hr)
            ar = layers[0, depth - 1, block, :]
            ai = layers[1, depth - 1, block, :]
            for j in range(depth - 1, -1, -1):
                ar, ai = ar * zr - ai * zi, ar * zi + ai * zr
                if j:
                    ar = ar + layers[0, j - 1, block, :]
                    ai = ai + layers[1, j - 1, block, :]
            out[0, f, block, :] = ar
            out[1, f, block, :] = ai


def gradient_kernel(pieces, sent, heard, out):
    freqs, rows = pieces.shape[1:3]
    depth = out.shape[1]
    for start in range(0, rows, 8):
        block = slice(start, start + 8)
        sums = [None] * depth
        for f in range(freqs):
            hr = heard[0, f : f + 1, :]
            hi = heard[1, f : f + 1, :]
            sr = sent[0, block, f : f + 1]
            si = sent[1, block, f : f + 1]
            zr = sr * hr - si * hi
            zi = sr * hi + si * hr
            tr = step_size * pieces[0, f, block, :]
            ti = step_size * pieces[1, f, block, :]
            for j in range(depth):
                tr, ti = tr * zr - ti * zi, tr * zi + ti * zr
                if f:
                    sums[j] = (sums[j][0] + tr, sums[j][1] + ti)
                else:
                    sums[j] = (tr, ti)
        for j in range(depth):
            out[0, j, block, :] = sums[j][0]
            out[1, j, block, :] = sums[j][1]


def pointwise(kernel, values, sent, heard, planes):
    _, count, rows, width = values.shape
    freqs = heard.shape[1]
    height = min(rows, 32)
    lanes = min(width, 128)
    return pl.pallas_call(
        kernel,
        grid=(rows // height, width // lanes),
        in_specs=[
            pl.BlockSpec((2, count, height, lanes), lambda i, k: (0, 0, i, k)),
            pl.BlockSpec((2, height, freqs), lambda i, k: (0, i, 0)),
            pl.BlockSpec((2, freqs, lanes), lambda i, k: (0, 0, k)),
        ],
        out_specs=pl.BlockSpec((2, planes, height, lanes), lambda i, k: (0, 0, i, k)),
        out_shape=jax.ShapeDtypeStruct((2, planes, rows, width), jnp.float32),
    )(values, sent, heard)


def per_device(spectrum, measured, wavenumber, send_weight, hear_weight, aperture):
    _, depth_local, rows_sent, rows_heard = spectrum.shape
    freq_local = measured.shape[1]
    freq_total = wavenumber.shape[0]
    senders = lax.axis_size("tx")
    hearers = lax.axis_size("rx")
    layers = lax.axis_size("freq")
    depth = depth_local * layers
    total_sent = rows_sent * senders
    total_heard = rows_heard * hearers
    slab = rows_sent // layers
    strip = rows_heard // senders
    band = rows_sent // hearers

    first_row = lax.axis_index("tx") * rows_sent + lax.axis_index("freq") * slab
    sent_phase = depth_step * roots(wavenumber, first_row, slab, total_sent).T
    heard_phase = depth_step * roots(wavenumber, lax.axis_index("rx") * rows_heard, rows_heard, total_heard)
    sent = jnp.stack([jnp.cos(sent_phase), jnp.sin(sent_phase)])
    heard = jnp.stack([jnp.cos(heard_phase), jnp.sin(heard_phase)])
    tables_sent = dft_tables(total_sent)
    tables_heard = tables_sent if total_heard == total_sent else dft_tables(total_heard)
    near = "qsm,qcfmw->qscfw"
    far = "qsm,qcfwm->qscfw"

    split = spectrum.reshape(2, depth_local, layers, slab, rows_heard)
    split = exchange(jnp.transpose(split, (2, 0, 1, 3, 4)), "freq")
    stacked = jnp.transpose(split, (1, 0, 2, 3, 4)).reshape(2, depth, slab, rows_heard)
    pair = pointwise(pair_kernel, stacked, sent, heard, freq_total)

    pair = pair.reshape(2, layers, freq_local, slab, senders, strip)
    pair = jnp.transpose(pair, (4, 1, 0, 2, 3, 5)).reshape(senders * layers, 2, freq_local, slab, strip)
    pair = exchange(pair, ("tx", "freq"))
    done = dft(quarters(pair, 2), tables_sent, near, 1.0)
    done = exchange(unmix(done, (senders * hearers,)), ("tx", "rx"))
    done = done.reshape((senders, hearers) + done.shape[1:])
    done = jnp.swapaxes(done, 0, 1).reshape((senders * hearers,) + done.shape[2:])
    done = dft(quarters(done, 3), tables_heard, far, 1.0)
    done = exchange(unmix(done, (hearers,)), "rx")
    field = jnp.transpose(done, (1, 2, 0, 4, 3)).reshape(2, freq_local, rows_sent, rows_heard)

    tiles_sent, tiles_heard = aperture.shape
    gate = aperture.astype(jnp.float32)
    weights = (
        send_weight.reshape(tiles_sent, -1)[:, :, None, None]
        * gate[:, None, :, None]
        * hear_weight.reshape(tiles_heard, -1)[None, None, :, :]
    ).reshape(rows_sent, rows_heard)
    residual = weights[None, None] * (measured - field)

    back = residual.reshape(2, freq_local, hearers, band, rows_heard)
    back = exchange(jnp.transpose(back, (2, 0, 1, 3, 4)), "rx")
    done = dft(quarters(back, 3), tables_heard, far, -1.0)
    done = unmix(done, (hearers, senders))
    done = jnp.swapaxes(done, 0, 1).reshape((senders * hearers,) + done.shape[2:])
    done = exchange(done, ("tx", "rx"))
    done = dft(quarters(done, 3), tables_sent, far, -1.0)
    done = exchange(unmix(done, (senders * layers,)), ("tx", "freq"))
    done = done.reshape(senders, layers, 2, freq_local, slab, strip)
    pieces = jnp.transpose(done, (2, 1, 3, 4, 0, 5)).reshape(2, freq_total, slab, rows_heard)

    gradient = pointwise(gradient_kernel, pieces, sent, heard, depth)
    gradient = gradient.reshape(2, layers, depth_local, slab, rows_heard)
    gradient = exchange(jnp.transpose(gradient, (1, 0, 2, 3, 4)), "freq")
    gradient = jnp.transpose(gradient, (1, 2, 0, 3, 4)).reshape(spectrum.shape)
    return (spectrum + gradient, residual)


lanes = 128
chunks = 2
mesh_ids = pl.DeviceIdType.MESH


def split(values):
    high = values.astype(jnp.bfloat16)
    return high, (values - high.astype(jnp.float32)).astype(jnp.bfloat16)


def multiply(left, right):
    return jnp.dot(left, right, preferred_element_type=jnp.float32)


def turned(base, high, low, left):
    def times(values, kind):
        return multiply(base[kind], values) if left else multiply(values, base[kind])

    first = times(high, 0) + (times(high, 1) + times(low, 0))
    second = times(high, 2) + (times(high, 3) + times(low, 2))
    return first, second


def moved_exactly(values, table):
    high = values.astype(jnp.bfloat16)
    rest = values - high.astype(jnp.float32)
    middle = rest.astype(jnp.bfloat16)
    low = (rest - middle.astype(jnp.float32)).astype(jnp.bfloat16)
    return (multiply(high, table) + multiply(middle, table)) + multiply(low, table)


def mix(parts, sign):
    (ar, ai), (br, bi), (cr, ci), (dr, di) = parts
    er, ei, gr, gi = ar + cr, ai + ci, ar - cr, ai - ci
    hr, hi, kr, ki = br + dr, bi + di, sign * (br - dr), sign * (bi - di)
    return (er + hr, ei + hi), (gr - ki, gi + kr), (er - hr, ei - hi), (gr + ki, gi - kr)


def aligned(index, size):
    return pl.ds(pl.multiple_of(index * size, size), size)


def phase_of(sent, heard, f, rows, columns):
    hr, hi = heard[0, f : f + 1, columns], heard[1, f : f + 1, columns]
    sr, si = sent[0, rows, f : f + 1], sent[1, rows, f : f + 1]
    return sr * hr - si * hi, sr * hi + si * hr


def halves(first, second):
    low = lax.broadcasted_iota(jnp.int32, first.shape, 1) < lanes // 2
    turn = lambda x: pltpu.roll(x, lanes // 2, 1)
    return jnp.where(low, first, turn(second)), jnp.where(low, turn(first), second)


def whole_kernel(sizes, refs):
    senders, hearers, layers, local, per = sizes
    spectrum, measured, weights, wavenumber = refs[:4]
    moved, residual, seen = refs[4:7]
    pieces, box, message, high, low, field, echo, weight = refs[7:15]
    sent, heard, base, turn_row, turn_column, order, order_back = refs[15:22]
    (in_got, in_sent, pair_got, pair_sent, back_got, back_sent, out_got, out_sent) = refs[22:30]
    (weight_got, weight_sent, seen_got, seen_sent, load, kept, left_sent, left_got, again) = refs[30:]
    groups = hearers * layers
    devices = senders * groups
    slab, wide = spectrum.shape[2:]
    tall = measured.shape[2]
    strip = wide // senders
    rows = slab // chunks
    spans = strip // lanes
    width = high.shape[1]
    planes = 2 * per
    block = layers * rows
    tx, rx, fq = lax.axis_index("tx"), lax.axis_index("rx"), lax.axis_index("freq")
    mine = rx * layers + fq
    me = tx * groups + mine

    def chunk(n):
        return pl.ds(n * rows, rows)

    def remote(source, target, send, receive, device):
        pltpu.make_async_remote_copy(
            src_ref=source, dst_ref=target, send_sem=send, recv_sem=receive, device_id=device, device_id_type=mesh_ids
        ).start()

    def near(source, target, sem):
        pltpu.make_async_copy(source, target, sem).start()

    def settle(ref, sem):
        pltpu.make_async_copy(ref, ref, sem).wait()

    def to_group(make, send, receive):
        def far(d, carry):
            j = lax.rem(fq + d, layers)
            for there in ((rx + 2) % hearers, 3 - rx, rx + 1 - 2 * (rx % 2)):
                for source, target in make(there * layers + j):
                    remote(source, target, send, receive, (tx, there, j))
            return carry

        def close(d, carry):
            j = lax.rem(fq + d, layers)
            for source, target in make(rx * layers + j):
                remote(source, target, send, receive, (tx, rx, j))
            return carry

        lax.fori_loop(0, layers, far, 0)
        lax.fori_loop(1, layers, close, 0)
        for source, target in make(mine):
            near(source, target, receive)

    def to_all(make, send, receive):
        def place(j, there):
            return (j // layers * hearers + there) * layers + j % layers

        def far(d, carry):
            j = lax.rem(tx * layers + fq + d, senders * layers)
            for there in ((rx + 2) % hearers, 3 - rx, rx + 1 - 2 * (rx % 2)):
                source, target = make(place(j, there))
                remote(source, target, send, receive, (j // layers, there, j % layers))
            return carry

        def close(d, carry):
            j = lax.rem(tx * layers + fq + d, senders * layers)
            source, target = make(place(j, rx))
            remote(source, target, send, receive, (j // layers, rx, j % layers))
            return carry

        lax.fori_loop(0, senders * layers, far, 0)
        lax.fori_loop(1, senders * layers, close, 0)
        source, target = make(me)
        near(source, target, receive)

    def pair_of(f, k):
        return pl.ds((f * devices + k) * 2, 2)

    def many(f):
        return pl.ds(f * devices * 2, devices * 2)

    for n in range(chunks):
        to_group(
            lambda g: [(spectrum.at[:, g, chunk(n), :], moved.at[:, mine, chunk(n), :])], in_sent.at[n], in_got.at[n]
        )
    for shift in range(senders):
        other = lax.rem(tx + shift, senders)
        for lc in range(spans):
            source = weights.at[:, aligned(other * spans + lc, lanes)]
            target = weight.at[lc, aligned(tx, tall), :]
            if shift:
                remote(source, target, weight_sent, weight_got, (other, rx, fq))
            else:
                near(source, target, weight_got)
        if shift:
            remote(
                measured.at[:, :, :, aligned(other, strip)],
                seen.at[shift - 1],
                seen_sent,
                seen_got,
                (other, rx, fq),
            )

    total = width * radix

    def make_phases(ref, numbers, offset, axis, shape):
        indices = offset + lax.broadcasted_iota(jnp.int32, shape, axis)
        signed = jnp.where(indices < total // 2, indices, indices - total)
        waves = 2.0 * jnp.pi / total * signed.astype(jnp.float32)
        phase = depth_step * jnp.sqrt(jnp.maximum(numbers * numbers - waves * waves, 0.0) + root_floor)
        ref[0], ref[1] = jnp.cos(phase), jnp.sin(phase)

    def make_tables():
        numbers = wavenumber[...]
        freqs = numbers.shape[1]
        square = (freqs, freqs)
        same = lax.broadcasted_iota(jnp.int32, square, 0) == lax.broadcasted_iota(jnp.int32, square, 1)
        tall_numbers = jnp.sum(jnp.where(same, jnp.broadcast_to(numbers, square), 0.0), axis=1, keepdims=True)
        make_phases(sent, numbers, tx * tall + mine * slab, 0, (slab, freqs))
        make_phases(heard, tall_numbers, 0, 1, (freqs, total))
        scale = 1.0 / math.sqrt(total)

        def angles(product, period):
            return 2.0 * math.pi / period * product.astype(jnp.float32)

        def fill(t, carry):
            down = aligned(t, 16)
            row = t * 16 + lax.broadcasted_iota(jnp.int32, (16, width), 0)
            product = jnp.bitwise_and(row * lax.broadcasted_iota(jnp.int32, (16, width), 1), width - 1)
            phase = angles(product, width)
            for k, values in enumerate((jnp.cos(phase), jnp.sin(phase))):
                base[2 * k, down, :], base[2 * k + 1, down, :] = split(values)
            row = row[:, :lanes]
            for s in range(radix):
                phase = angles(s * row, total)
                turn_column[2 * s, down, :] = jnp.cos(phase) * scale
                turn_column[2 * s + 1, down, :] = jnp.sin(phase) * scale
            return carry

        lax.fori_loop(0, width // 16, fill, 0)
        for s in range(radix):
            phase = angles(s * lax.broadcasted_iota(jnp.int32, (1, width), 1), total)
            turn_row[2 * s : 2 * s + 1, :] = jnp.cos(phase) * scale
            turn_row[2 * s + 1 : 2 * s + 2, :] = jnp.sin(phase) * scale
        part = strip // radix
        for ref, axis in ((order, 0), (order_back, 1)):
            natural = lax.broadcasted_iota(jnp.int32, (strip, strip), axis)
            place = lax.broadcasted_iota(jnp.int32, (strip, strip), 1 - axis)
            source = jnp.bitwise_and(place, part - 1) * radix + place // part
            ref[...] = jnp.where(natural == source, 1.0, 0.0).astype(jnp.bfloat16)

    make_tables()

    def make_pairs(f, n):
        for g in range(layers):

            def body(t, carry):
                row, span = t // (wide // lanes), t % (wide // lanes)
                down, across = aligned(n * (rows // 16) + row, 16), aligned(span, lanes)
                parts = []
                for h in range(hearers):
                    where = aligned(h * (wide // lanes) + span, lanes)
                    zr, zi = phase_of(sent, heard, g * local + f, down, where)
                    ar = moved[per - 1, h * layers + layers - 1, down, across]
                    ai = moved[planes - 1, h * layers + layers - 1, down, across]
                    for j in range(layers * per - 1, -1, -1):
                        ar, ai = ar * zr + ai * zi, ai * zr - ar * zi
                        if j:
                            q, d = divmod(j - 1, per)
                            ar = ar + moved[d, h * layers + q, down, across]
                            ai = ai + moved[per + d, h * layers + q, down, across]
                    parts.append((ar, ai))
                for s, (real, imag) in enumerate(mix(parts, 1.0)):
                    cr, ci = turn_row[2 * s : 2 * s + 1, across], turn_row[2 * s + 1 : 2 * s + 2, across]
                    for c, value in enumerate((real * cr - imag * ci, real * ci + imag * cr)):
                        place = aligned((c * block + g * rows) // 16 + row, 16)
                        high[s, place, across], low[s, place, across] = split(value)
                return carry

            lax.fori_loop(0, rows // 16 * (wide // lanes), body, 0)

        def turn(s, carry):
            first, second = turned(base, high[s, : 2 * block, :], low[s, : 2 * block, :], False)
            field[s, :block, :] = first[:block] - second[block:]
            field[s, block : 2 * block, :] = first[block:] + second[:block]
            return carry

        lax.fori_loop(0, radix, turn, 0)
        for c in range(2):
            for g in range(layers):
                down = pl.ds(c * block + g * rows, rows)
                for p in range(hearers):
                    across = pl.ds(p * lanes, lanes)
                    for lc in range(spans):
                        values = halves(field[2 * lc, down, across], field[2 * lc + 1, down, across])
                        for k in range(senders):
                            place = (f * devices + (k * hearers + p) * layers + g) * 2 + c
                            message[place, chunk(n), lc * lanes : (lc + 1) * lanes] = values[k]

    def send_pairs(f, n):
        to_all(
            lambda k: (message.at[pair_of(f, k), chunk(n), :], box.at[pair_of(f, me), chunk(n), :]),
            pair_sent.at[f, n],
            pair_got.at[f, n],
        )

    def load_echo(f):
        for c in range(2):
            for lc in range(spans):
                for shift in range(senders):
                    source = (
                        seen.at[shift - 1, c, f, :, pl.ds(lc * lanes, lanes)]
                        if shift
                        else measured.at[c, f, :, aligned(tx * spans + lc, lanes)]
                    )
                    other = lax.rem(tx + senders - shift, senders)
                    near(source, echo.at[f, c, lc, aligned(other, tall), :], load.at[f])

    def send_left(f):
        for c in range(2):
            for lc in range(spans):
                for shift in range(senders):
                    other = lax.rem(tx + senders - shift, senders)
                    source = echo.at[f, c, lc, aligned(other, tall), :]
                    target = residual.at[c, f, :, aligned(tx * spans + lc, lanes)]
                    if shift:
                        remote(source, target, left_sent.at[f], left_got.at[f], (other, rx, fq))
                    else:
                        near(source, target, kept.at[f])

    def settle_left(f):
        settle(echo.at[f, :, :, pl.ds(0, tall), :], kept.at[f])
        settle(echo.at[f, :, :, pl.ds(tall, tall * (senders - 1)), :], left_sent.at[f])

    quarter = devices // radix

    def columns(f):
        def gather(t, carry):
            d, row = t // (slab // 16), t % (slab // 16)
            here, down = aligned(row, 16), aligned(t, 16)
            for lc in range(spans):
                across = slice(lc * lanes, (lc + 1) * lanes)
                parts = [
                    tuple(box[(f * devices + q * quarter + d) * 2 + c, here, across] for c in range(2))
                    for q in range(radix)
                ]
                for s, (real, imag) in enumerate(mix(parts, 1.0)):
                    cr, ci = turn_column[2 * s, down, :], turn_column[2 * s + 1, down, :]
                    for c, value in enumerate((real * cr - imag * ci, real * ci + imag * cr)):
                        place = slice(c * strip + lc * lanes, c * strip + (lc + 1) * lanes)
                        high[s, down, place], low[s, down, place] = split(value)
            return carry

        lax.fori_loop(0, width // 16, gather, 0)

        def middle(s, carry):
            first, second = turned(base, high[s], low[s], True)
            picked = pl.ds(s, width, stride=radix)
            for c in range(2):
                if c:
                    value = first[:, strip:] + second[:, :strip]
                else:
                    value = first[:, :strip] - second[:, strip:]
                value = moved_exactly(value, order_back[...])
                left = []
                for lc in range(spans):
                    across = slice(lc * lanes, (lc + 1) * lanes)
                    part = weight[lc, picked, :] * (echo[f, c, lc, picked, :] - value[:, across])
                    echo[f, c, lc, picked, :] = part
                    left.append(part)
                parts = split(jnp.concatenate(left, axis=1))
                for ref, part in zip((high, low), parts):
                    ref[s, :, c * strip : (c + 1) * strip] = multiply(part, order[...]).astype(jnp.bfloat16)
            first, second = turned(base, high[s], low[s], True)
            field[s, :, :strip] = first[:, :strip] + second[:, strip:]
            field[s, :, strip:] = first[:, strip:] - second[:, :strip]
            return carry

        lax.fori_loop(0, radix, middle, 0)

        def scatter(t, carry):
            d, row = t // (slab // 16), t % (slab // 16)
            here, down = aligned(row, 16), aligned(t, 16)
            for lc in range(spans):
                across = slice(lc * lanes, (lc + 1) * lanes)
                parts = []
                for s in range(radix):
                    real = field[s, down, lc * lanes : (lc + 1) * lanes]
                    imag = field[s, down, strip + lc * lanes : strip + (lc + 1) * lanes]
                    cr, ci = turn_column[2 * s, down, :], turn_column[2 * s + 1, down, :]
                    parts.append((real * cr + imag * ci, imag * cr - real * ci))
                for q, values in enumerate(mix(parts, -1.0)):
                    for c in range(2):
                        message[(f * devices + q * quarter + d) * 2 + c, here, across] = values[c]
            return carry

        lax.fori_loop(0, width // 16, scatter, 0)

    def send_back(f, n):
        to_all(
            lambda k: (message.at[pair_of(f, k), chunk(n), :], pieces.at[pair_of(f, me), chunk(n), :]),
            back_sent.at[f, n],
            back_got.at[f, n],
        )

    def gradient(f, n):
        for c in range(2):
            for g in range(layers):
                down = pl.ds(c * block + g * rows, rows)
                for p in range(hearers):
                    for lc in range(spans):
                        across = slice(lc * lanes, (lc + 1) * lanes)
                        where = [(f * devices + (k * hearers + p) * layers + g) * 2 + c for k in range(senders)]
                        values = halves(*[pieces[k, chunk(n), across] for k in where])
                        for k in range(2):
                            spot = (2 * lc + k, down, pl.ds(p * lanes, lanes))
                            high[spot], low[spot] = split(values[k])

        def turn(s, carry):
            first, second = turned(base, high[s, : 2 * block, :], low[s, : 2 * block, :], False)
            field[s, :block, :] = first[:block] + second[block:]
            field[s, block : 2 * block, :] = first[block:] - second[:block]
            return carry

        lax.fori_loop(0, radix, turn, 0)

        def body(t, carry):
            row, span = t // (wide // lanes), t % (wide // lanes)
            across = aligned(span, lanes)
            for g in range(layers):
                spots = [aligned((c * block + g * rows) // 8 + row, 8) for c in range(2)]
                parts = []
                for s in range(radix):
                    real, imag = field[s, spots[0], across], field[s, spots[1], across]
                    cr, ci = turn_row[2 * s : 2 * s + 1, across], turn_row[2 * s + 1 : 2 * s + 2, across]
                    parts.append((real * cr + imag * ci, imag * cr - real * ci))
                for h, values in enumerate(mix(parts, -1.0)):
                    for c in range(2):
                        field[h, spots[c], across] = step_size * values[c]
            here = aligned(n * (rows // 8) + row, 8)
            inner = aligned(span % spans, lanes)
            for h in range(hearers):
                sums = [None] * (layers * per)
                for g in range(layers):
                    where = aligned(h * (wide // lanes) + span, lanes)
                    zr, zi = phase_of(sent, heard, g * local + f, here, where)
                    tr, ti = [field[h, aligned((c * block + g * rows) // 8 + row, 8), across] for c in range(2)]
                    for j in range(layers * per):
                        tr, ti = tr * zr - ti * zi, tr * zi + ti * zr
                        sums[j] = (sums[j][0] + tr, sums[j][1] + ti) if g else (tr, ti)
                for j in range(layers * per):
                    q, d = divmod(j, per)
                    for c in range(2):
                        place = ((h * layers + q) * senders + span // spans) * planes + c * per + d
                        value = sums[j][c]
                        if f:
                            value = value + box[place, here, inner]
                        box[place, here, inner] = value
            return carry

        lax.fori_loop(0, rows // 8 * (wide // lanes), body, 0)

    def send_out(n):
        to_group(
            lambda g: [
                (
                    box.at[pl.ds((g * senders + k) * planes, planes), chunk(n), :],
                    moved.at[:, mine, chunk(n), pl.ds(k * strip, strip)],
                )
                for k in range(senders)
            ],
            out_sent.at[n],
            out_got.at[n],
        )

    for n in range(chunks):
        settle(moved.at[:, :, chunk(n), :], in_got.at[n])
        make_pairs(0, n)
        send_pairs(0, n)
        if n:
            for k in range(n):
                for f in range(1, local):
                    send_pairs(f, k)
        for f in range(1, local):
            make_pairs(f, n)
    for f in range(1, local):
        send_pairs(f, chunks - 1)
    settle(weight, weight_got)
    settle(seen, seen_got)
    for f in range(local):
        load_echo(f)
    for f in range(local):
        settle(echo.at[f], load.at[f])
        for n in range(chunks):
            settle(box.at[many(f), chunk(n), :], pair_got.at[f, n])
            settle(message.at[pl.ds(0, (devices - 1) * 2), chunk(n), :], pair_sent.at[f, n])
        columns(f)
        for n in range(chunks):
            send_back(f, n)
    for f in range(local):
        send_left(f)
    for f in range(local):
        for n in range(chunks):
            settle(pieces.at[many(f), chunk(n), :], back_got.at[f, n])
            gradient(f, n)
            if f == local - 1:
                send_out(n)
    for n in range(chunks):
        for p in range(planes):
            for k in range(senders):
                near(
                    spectrum.at[p, :, chunk(n), pl.ds(k * strip, strip)],
                    pieces.at[pl.ds((p * senders + k) * groups, groups), chunk(n), :],
                    again.at[n],
                )
    for n in range(chunks):
        settle(pieces.at[:, chunk(n), :], again.at[n])
        settle(moved.at[:, :, chunk(n), :], out_got.at[n])

        def add(t, carry):
            p, g = t // groups, t % groups
            for k in range(senders):
                across = slice(k * strip, (k + 1) * strip)
                moved[p, g, chunk(n), across] += pieces[(p * senders + k) * groups + g, chunk(n), :]
            return carry

        lax.fori_loop(0, planes * groups, add, 0)
    for f in range(local):
        settle_left(f)
    for n in range(chunks):
        settle(spectrum.at[:, pl.ds(0, groups - 1), chunk(n), :], in_sent.at[n])
        for f in range(local):
            settle(message.at[pl.ds(0, (devices - 1) * 2), chunk(n), :], back_sent.at[f, n])
        settle(box.at[pl.ds(0, (groups - 1) * senders * planes), chunk(n), :], out_sent.at[n])
    settle(weights.at[:, pl.ds(0, strip * (senders - 1))], weight_sent)
    settle(seen, seen_sent)
    for f in range(local):
        settle(residual.at[:, f, :, pl.ds(0, strip * (senders - 1))], left_got.at[f])


def per_device_whole(spectrum, measured, wavenumber, send_weight, hear_weight, aperture):
    _, per, rows_sent, rows_heard = spectrum.shape
    local = measured.shape[1]
    senders = lax.axis_size("tx")
    hearers = lax.axis_size("rx")
    layers = lax.axis_size("freq")
    total = rows_sent * senders
    groups = hearers * layers
    slab = rows_sent // groups
    strip = rows_heard // senders
    width = total // radix

    tiles_sent, tiles_heard = aperture.shape
    gate = jnp.repeat(aperture.astype(jnp.float32), rows_heard // tiles_heard, axis=1) * hear_weight[None, :]
    weights = gate[:, None, :] * send_weight.reshape(tiles_sent, -1)[:, :, None]
    weights = weights.reshape(rows_sent, rows_heard)

    sizes = (senders, hearers, layers, local, per)
    anywhere = pl.BlockSpec(memory_space=pl.ANY)
    inside = pl.BlockSpec(memory_space=pltpu.VMEM)
    count = local * senders * groups * 2
    freqs = local * layers
    blocks = spectrum.reshape(2 * per, groups, slab, rows_heard)
    floats = lambda *shape: pltpu.VMEM(shape, jnp.float32)
    sems = pltpu.SemaphoreType.DMA
    moved, residual, _ = pl.pallas_call(
        lambda *refs: whole_kernel(sizes, refs),
        in_specs=[anywhere] * 3 + [inside],
        out_specs=[inside] + [anywhere] * 2,
        out_shape=[
            pltpu.VMEM(blocks.shape, jnp.float32),
            jax.ShapeDtypeStruct(measured.shape, jnp.float32),
            jax.ShapeDtypeStruct((senders - 1, 2, local, rows_sent, strip), jnp.float32),
        ],
        scratch_shapes=[
            floats(count, slab, strip),
            floats(count, slab, strip),
            floats(count, slab, strip),
            pltpu.VMEM((radix, width, width), jnp.bfloat16),
            pltpu.VMEM((radix, width, width), jnp.bfloat16),
            floats(radix, width, width),
            floats(local, 2, strip // lanes, total, lanes),
            floats(strip // lanes, total, lanes),
            floats(2, slab, freqs),
            floats(2, freqs, total),
            pltpu.VMEM((4, width, width), jnp.bfloat16),
            floats(2 * radix, width),
            floats(2 * radix, width, lanes),
            pltpu.VMEM((strip, strip), jnp.bfloat16),
            pltpu.VMEM((strip, strip), jnp.bfloat16),
        ]
        + [sems((chunks,))] * 2
        + [sems((local, chunks))] * 4
        + [sems((chunks,))] * 2
        + [sems] * 4
        + [sems((local,))] * 4
        + [sems((chunks,))],
        compiler_params=pltpu.CompilerParams(vmem_limit_bytes=limit, has_side_effects=True),
    )(blocks, measured, weights, wavenumber.reshape(1, -1))
    return (moved.reshape(spectrum.shape), residual)


def fits(mesh, sent, heard):
    senders, hearers, layers = [mesh.shape[axis] for axis in ("tx", "rx", "freq")]
    rows = sent // senders // (hearers * layers)
    return (
        hearers == radix
        and senders == 2
        and sent == heard
        and rows % (16 * chunks) == 0
        and heard // hearers // radix == lanes
        and heard & (heard - 1) == 0
    )


def solution(mesh):
    placed = (
        P(None, "freq", "tx", "rx"),
        P(None, "freq", "tx", "rx"),
        P(),
        P("tx"),
        P("rx"),
        P("tx", "rx"),
    )

    def body(*args):
        sent, heard = args[3].shape[0] * mesh.shape["tx"], args[4].shape[0] * mesh.shape["rx"]
        return (per_device_whole if fits(mesh, sent, heard) else per_device)(*args)

    return jax.shard_map(
        body,
        mesh=mesh,
        in_specs=placed,
        out_specs=(P(None, "freq", "tx", "rx"), P(None, "freq", "tx", "rx")),
        check_vma=False,
    )
```
